128 devices in a mesh: gx: 8 (over z_lo, x), gy: 16 (over y, z_hi, core).
Axes of the slice: x: 4, y: 4, z: 4 (z_hi: 2, z_lo: 2; z = z_hi * 2 + z_lo), core: 2. Of those that a mesh axis runs over, the one named last changes fastest.
Arguments:
- displacement: float32 [3, 16, 32, 3, 128], P(None, 'gx', 'gy'), may hold values from -0.15 to 0.15
- velocity: float32 [3, 16, 32, 3, 128], P(None, 'gx', 'gy'), may hold values from -18 to 18
- noise: float32 [4, 3, 16, 32, 3, 128], P(None, None, 'gx', 'gy'), may hold values from -1.7320508 to 1.7320508
- electron_temp: float32 [128, 8, 16], P(('gx', 'gy')), may hold values from 0.5 to 10
- pair_list: int32 [8, 16, 2, 324], P('gx', 'gy'), may hold values from 0 to 26, as said below
- pair_count: int32 [8, 16], P('gx', 'gy'), may hold values from 12 to 324, as said below
Outputs:
- new_displacement: float32 [3, 16, 32, 3, 128], P(None, 'gx', 'gy')
- new_velocity: float32 [3, 16, 32, 3, 128], P(None, 'gx', 'gy')
- electron_final: float32 [128, 8, 16], P(('gx', 'gy'))
The draws below stay inside these ranges and needn't reach their ends.
Inputs may be any that keep to these rules, and one draw needn't show every extreme that they name: `pair_list`: in each brick the first pair_count entries name distinct (tile, code) pairs, the tile in 0 to 11 and the code in 0 to 26; every tile's code 13 is among them. Later entries are not read. `pair_count`: some brick has exactly 324 live entries and some brick exactly 12.
All inputs are finite; a program needn't handle non-finite values.
Results may differ from the reference program's by a relative error of at most 0.0003.
Values sent between devices are 32-bit elements; how exact they have to be, the bound alone decides.
A program may use at most 64 MiB of HBM per device.

```python
import math
from functools import partial
import jax
import jax.numpy as jnp
from jax import lax

CB = 4
TILE = 128
BXT = 2
BYT = 2
TZ = 3
TILES = 12
PAIRS = 324
STEPS = 4
SUB = 6
NXG = 8
NYG = 16
NZG = 128
N_GX = 8
N_GY = 16


def brick_lists(key):
    inner = jax.random.fold_in(key, 31)
    bricks = N_GX * N_GY
    keys = jax.random.split(inner, bricks + 2)
    spread = jax.random.randint(keys[0], (bricks,), 0, 1024)
    extra = (PAIRS - TILES) * spread * spread // (1023 * 1023)
    busiest = jax.random.randint(keys[1], (), 0, bricks)
    serial = jnp.arange(bricks)
    totals = jnp.where(serial == busiest, PAIRS, TILES + extra)
    totals = jnp.where(serial == (busiest + 1) % bricks, TILES, totals)
    others = jnp.arange(26 * TILES)
    other_tile = others // 26
    other_rank = others % 26
    other_code = other_rank + (other_rank >= 13).astype(other_rank.dtype)
    orders = jax.vmap(lambda brick_key: jax.random.permutation(brick_key, 26 * TILES))(keys[2:])
    own_tiles = jnp.broadcast_to(jnp.arange(TILES), (bricks, TILES))
    tiles_row = jnp.concatenate([own_tiles, other_tile[orders]], axis=1)
    codes_row = jnp.concatenate([jnp.full((bricks, TILES), 13, dtype=other_code.dtype), other_code[orders]], axis=1)
    table = jnp.stack([tiles_row, codes_row], axis=1).reshape(N_GX, N_GY, 2, PAIRS).astype(jnp.int32)
    return (table, totals.reshape(N_GX, N_GY).astype(jnp.int32))


def draw_pair_list(key, part):
    return brick_lists(key)[0]


def draw_pair_count(key, part):
    return brick_lists(key)[1]


def draw_velocity(key, part):
    shape = (3, BXT * N_GX, BYT * N_GY, TZ, TILE)
    inner = jax.random.fold_in(key, 57)
    sign_key, size_key = jax.random.split(inner)
    signs = (jax.random.randint(sign_key, shape, 0, 2) * 2 - 1).astype(jnp.float32)
    magnitude = jax.random.uniform(size_key, shape, jnp.float32, 12.0, 18.0)
    return (signs * magnitude).astype(jnp.float32)


def levels(stream_key, shape, cuts, smallest, high):
    level, own = 1.0, jax.random.fold_in(stream_key, 6)
    for dim, parts in cuts:
        steps = jnp.exp(jax.random.uniform(jax.random.fold_in(own, dim), (parts,), jnp.float32, smallest / len(cuts), high / len(cuts)))
        level = level * jnp.repeat(steps, shape[dim] // parts).reshape([-1 if axis == dim else 1 for axis in range(len(shape))])
    return level


def setup_inputs(seed: int = 0) -> dict:
    key_of = jax.random.split(jax.random.key(seed), 7)
    displacement = jnp.clip(jax.random.uniform(key_of[0], (3, BXT * N_GX, BYT * N_GY, TZ, TILE), jnp.float32, -0.15, 0.15) * levels(key_of[0], (3, BXT * N_GX, BYT * N_GY, TZ, TILE), ((1, 8), (2, 16)), -0.4, 0.0), -0.15, 0.15)
    velocity = draw_velocity(jax.random.fold_in(key_of[6], 71), 0)
    noise = jnp.clip(jax.random.uniform(key_of[2], (STEPS, 3, BXT * N_GX, BYT * N_GY, TZ, TILE), jnp.float32, -1.7320508, 1.7320508) * levels(key_of[2], (STEPS, 3, BXT * N_GX, BYT * N_GY, TZ, TILE), ((2, 8), (3, 16)), -0.4, 0.0), -1.7320508, 1.7320508)
    electron_temp = jnp.clip(jnp.exp(math.log(10.0) - 2.9957323 * jax.random.uniform(key_of[3], (NZG, NXG, NYG), jnp.float32) ** levels(key_of[3], (NZG, NXG, NYG), ((0, 128),), -0.2, 0.2)), 0.5, 10.0)
    pair_list = draw_pair_list(jax.random.fold_in(key_of[6], 71), 0)
    pair_count = draw_pair_count(jax.random.fold_in(key_of[6], 71), 0)
    return dict(displacement=displacement, velocity=velocity, noise=noise, electron_temp=electron_temp, pair_list=pair_list, pair_count=pair_count)


lattice_edge = 3.1652
density_cut = 4.400224
embed_scale = 1.896373
pair_cut = 3.25
coef_zero = 47.1346499
coef_one = -33.7665655
coef_two = 6.2541999
time_step = 0.005
atom_mass = 0.0190534
friction = 1.0
heat_capacity = 0.02
diffusion_rate = 0.12

def lattice_sites():
    serial = jnp.arange(TILE, dtype=jnp.int32)
    cell_number = serial // 2
    half_step = (serial % 2).astype(jnp.float32) * 0.5
    corners = jnp.stack([cell_number // (CB * CB), cell_number // CB % CB, cell_number % CB])
    return lattice_edge * (corners.astype(jnp.float32) + half_step[None, :])

def plane_table(plane_total):
    serial = jnp.arange(TILE, dtype=jnp.int32)
    cell_number = serial // 2
    layer = 2 * (cell_number % CB) + serial % 2
    tiles = jnp.arange(TZ, dtype=jnp.int32)
    whole = tiles[:, None] * (2 * CB) + layer[None, :]
    return (whole * plane_total // (2 * CB * TZ)).astype(jnp.int32)

def pair_geometry(window, tile_index, neighbour_code, lattice):
    wide_y = BYT + 2
    depth_t = tile_index % TZ
    inner_y = tile_index // TZ % BYT
    inner_x = tile_index // (TZ * BYT)
    shift_x = neighbour_code // 9
    shift_y = neighbour_code // 3 % 3
    shift_z = neighbour_code % 3
    flattened = window.reshape(window.shape[0], (BXT + 2) * wide_y * TZ, TILE)
    own_index = ((inner_x + 1) * wide_y + inner_y + 1) * TZ + depth_t
    other_index = ((inner_x + shift_x) * wide_y + inner_y + shift_y) * TZ + (depth_t + shift_z - 1 + TZ) % TZ
    own_tile = lax.dynamic_index_in_dim(flattened, own_index, 1, keepdims=False)
    other_tile = lax.dynamic_index_in_dim(flattened, other_index, 1, keepdims=False)
    offset = jnp.stack([shift_x - 1, shift_y - 1, shift_z - 1]).astype(jnp.float32) * (CB * lattice_edge)
    left = lattice + own_tile
    right = lattice + other_tile + offset[:, None]
    delta = left[:, :, None] - right[:, None, :]
    square = lax.optimization_barrier(jnp.sum(delta * delta, axis=0))
    serial = jnp.arange(TILE, dtype=jnp.int32)
    same_atom = (neighbour_code == 13) & (serial[:, None] == serial[None, :])
    distance = jnp.sqrt(jnp.where(same_atom, 100.0, square))
    return (delta, distance, own_index, other_index)

def density_term(window, lattice, tile_index, neighbour_code):
    delta, distance, own_index, other_index = pair_geometry(window, tile_index, neighbour_code, lattice)
    dens_gap = distance - density_cut
    return lax.optimization_barrier(jnp.sum(jnp.where(distance < density_cut, dens_gap * dens_gap, 0.0), axis=1))[None]

def force_term(window, embed_window, lattice, tile_index, neighbour_code):
    delta, distance, own_index, other_index = pair_geometry(window, tile_index, neighbour_code, lattice)
    flat_embed = embed_window.reshape((BXT + 2) * (BYT + 2) * TZ, TILE)
    own_embed = lax.dynamic_index_in_dim(flat_embed, own_index, 0, keepdims=False)
    other_embed = lax.dynamic_index_in_dim(flat_embed, other_index, 0, keepdims=False)
    pair_gap = distance - pair_cut
    poly = coef_zero + coef_one * distance + coef_two * distance * distance
    pair_slope = jnp.where(distance < pair_cut, 2.0 * pair_gap * poly + pair_gap * pair_gap * (coef_one + 2.0 * coef_two * distance), 0.0)
    dens_gap = distance - density_cut
    dens_slope = jnp.where(distance < density_cut, 2.0 * dens_gap, 0.0)
    scalar = (pair_slope + (own_embed[:, None] + other_embed[None, :]) * dens_slope) / distance
    return -lax.optimization_barrier(jnp.sum(scalar[None] * delta, axis=2))

def brick_total(term_fn, channels, pair_table, pair_total):
    initial = jnp.zeros((channels, TILES, TILE), jnp.float32)

    def visit(running, entry_index):
        tile_index = pair_table[0, entry_index]
        neighbour_code = pair_table[1, entry_index]
        term = term_fn(tile_index, neighbour_code)
        term = jnp.where(entry_index < pair_total, term, 0.0)
        return (running.at[:, tile_index].add(term), None)
    return lax.scan(visit, initial, jnp.arange(PAIRS, dtype=jnp.int32))[0]

def brick_density(window, pair_table, pair_total):
    return brick_total(partial(density_term, window, lattice_sites()), 1, pair_table, pair_total)

def brick_force(window, embed_window, pair_table, pair_total):
    return brick_total(partial(force_term, window, embed_window, lattice_sites()), 3, pair_table, pair_total)

def windows(values_in):
    channels = values_in.shape[0]
    padded = jnp.pad(values_in, ((0, 0), (1, 1), (1, 1), (0, 0), (0, 0)), mode='wrap')
    serial = jnp.arange(N_GX * N_GY, dtype=jnp.int32)

    def cut(brick):
        zero = jnp.zeros((), jnp.int32)
        starts = (zero, brick // N_GY * BXT, brick % N_GY * BYT, zero, zero)
        return lax.dynamic_slice(padded, starts, (channels, BXT + 2, BYT + 2, TZ, TILE))
    return jax.vmap(cut)(serial)

def from_bricks(per_brick):
    channels = per_brick.shape[1]
    shaped = per_brick.reshape(N_GX, N_GY, channels, BXT, BYT, TZ, TILE)
    return jnp.transpose(shaped, (2, 0, 3, 1, 4, 5, 6)).reshape(channels, N_GX * BXT, N_GY * BYT, TZ, TILE)

def to_bricks(values_in):
    channels = values_in.shape[0]
    shaped = values_in.reshape(channels, N_GX, BXT, N_GY, BYT, TZ, TILE)
    return jnp.transpose(shaped, (1, 3, 0, 2, 4, 5, 6)).reshape(N_GX * N_GY, channels, BXT, BYT, TZ, TILE)

def diffuse(heat):
    beside_all = jnp.roll(heat, 1, 0) + jnp.roll(heat, -1, 0) + jnp.roll(heat, 1, 1) + jnp.roll(heat, -1, 1)
    beside_all = beside_all + jnp.roll(heat, 1, 2) + jnp.roll(heat, -1, 2)
    return heat + diffusion_rate * (beside_all - 6.0 * heat)

def reference(displacement, velocity, noise, electron_temp, pair_list, pair_count):
    bricks = N_GX * N_GY
    positions = displacement
    speeds = velocity
    heat_field = electron_temp
    planes = plane_table(NZG).reshape(-1)
    pair_table = pair_list.reshape(bricks, 2, PAIRS)
    pair_total = pair_count.reshape(bricks)
    for step_index in range(STEPS):
        columns = jnp.transpose(heat_field.reshape(NZG, bricks))
        column_temp = jnp.take(columns, planes, axis=1).reshape(bricks, 1, 1, 1, TZ, TILE)
        local_temp = from_bricks(jnp.broadcast_to(column_temp, (bricks, 1, BXT, BYT, TZ, TILE)))[0]
        window = windows(positions)
        density = jax.vmap(brick_density)(window, pair_table, pair_total)
        density = from_bricks(density.reshape(bricks, 1, BXT, BYT, TZ, TILE))
        embed_slope = -embed_scale / (2.0 * jnp.sqrt(density))
        embed_window = windows(embed_slope)
        force = jax.vmap(brick_force)(window, embed_window, pair_table, pair_total)
        force = from_bricks(force.reshape(bricks, 3, BXT, BYT, TZ, TILE))
        kicker = jnp.sqrt(2.0 * friction * atom_mass * local_temp / time_step)[None] * noise[step_index]
        speeds = speeds + time_step / atom_mass * (force - friction * atom_mass * speeds + kicker)
        positions = positions + time_step * speeds
        power = friction * atom_mass * time_step * lax.optimization_barrier(jnp.sum(speeds * speeds, axis=0))
        brick_power = lax.optimization_barrier(jnp.sum(to_bricks(power[None])[:, 0], axis=(1, 2))).reshape(bricks, TZ * TILE)
        energy = jax.vmap(lambda values: jnp.zeros((NZG,), jnp.float32).at[planes].add(values))(brick_power)
        heat_field = heat_field + jnp.transpose(energy).reshape(NZG, N_GX, N_GY) / heat_capacity
        for sub_index in range(SUB):
            heat_field = diffuse(heat_field)
    return (positions, speeds, heat_field)
```

```python
from functools import partial

import jax
import jax.numpy as jnp
import numpy as np
from jax import lax
from jax.experimental import pallas as pl
from jax.experimental.pallas import tpu as pltpu
from jax.sharding import PartitionSpec as P

MESH = pl.DeviceIdType.MESH
NGX, NGY = 8, 16
TZ, TILE, TILES, STEPS, SUB = 3, 128, 12, 4, 6
PAIRS = 324

EDGE = 3.1652
RC = 4.400224
EMBED = 1.896373
RP = 3.25
C0, C1, C2 = 47.1346499, -33.7665655, 6.2541999
DT = 0.005
MASS = 0.0190534
HEAT = 0.02
RATE = 0.12

F32 = jnp.float32
PAD = 16
ROWS = 48
FLAT = PAD + ROWS + PAD

OFFSETS = sorted(
    (
        (nx, ny, nz)
        for nx in range(-3, 4)
        for ny in range(-3, 4)
        for nz in range(-3, 4)
        if nx % 2 == ny % 2 == nz % 2 and 0 < nx * nx + ny * ny + nz * nz <= 12
    ),
    key=lambda n: (n[0] ** 2 + n[1] ** 2 + n[2] ** 2 > 8, n[1], n[2], n[0]),
)
NEAR = 26
NEAR_LIMIT = 0.42**2
FAR_LIMIT = 0.96**2
SIDES = [(a, b) for a in (-1, 0, 1) for b in (-1, 0, 1) if (a, b) != (0, 0)]
HOPS = sorted(
    (
        (dx, dy, dz, dc)
        for dx in range(4)
        for dy in range(4)
        for dz in range(4)
        for dc in range(2)
        if (dx, dy, dz, dc) != (0, 0, 0, 0)
    ),
    key=lambda d: -sum(min(v, 4 - v) for v in d[:3]) * 2 - d[3],
)


def lane_tables():
    s = np.arange(TILE)
    cx, cy, hz = s // 32, s // 8 % 4, s % 8
    b = hz % 2
    source, code = [], []
    for nx, ny, nz in OFFSETS:
        odd = nx % 2
        dx = (nx - odd) // 2 + odd * b
        dy = (ny - odd) // 2 + odd * b
        source.append((cx + dx) % 4 * 32 + (cy + dy) % 4 * 8 + (hz + nz) % 8)
        code.append(9 * ((cx + dx) // 4 + 1) + 3 * ((cy + dy) // 4 + 1) + (hz + nz) // 8 + 1)
    table = np.stack(source + code).astype(np.int32)
    return np.ascontiguousarray(np.broadcast_to(table[:, None, :], (2 * len(OFFSETS), 8, TILE)))


def plane_tables():
    s = np.arange(TILE)
    layer = np.arange(8)[:, None] % 3 * 8 + s[None, :] % 8
    plane = layer * 128 // 24
    back = np.zeros((8, TILE), np.int32)
    live = np.zeros((8, TILE), np.int32)
    for L in range(24):
        back[L // 8, L * 128 // 24] = L % 8
        live[L // 8, L * 128 // 24] = 1
    return np.stack([plane, back, live]).astype(np.int32)


def spread(x, index):
    return jnp.take_along_axis(x, index, axis=1, mode="promise_in_bounds")


def body(
    u_in, v_in, noise, heat_in, pairs, count, lanes, planes,
    u_out, v_out, heat_out, flag_out,
    own, arrive, grid, row, win, zed, wye, mask, live_win, vel, kick, field,
    halo_send, halo_recv, all_send, all_recv, junk,
):
    mx, my = lax.axis_index("gx"), lax.axis_index("gy")
    x, zl = lax.rem(mx, 4), mx // 4
    y, zh, core = my // 4, lax.rem(my // 2, 2), lax.rem(my, 2)
    z = zh * 2 + zl
    xs = [lax.rem(x + d, 4) for d in range(4)]
    ys = [lax.rem(y + d, 4) for d in range(4)]
    zs = [lax.rem(z + d, 4) for d in range(4)]
    cs = [lax.rem(core + d, 2) for d in range(2)]
    gxs = {(dx, dz): lax.rem(zs[dz], 2) * 4 + xs[dx] for dx in range(4) for dz in range(4)}
    gys = {
        (dy, dz, dc): ys[dy] * 4 + zs[dz] // 2 * 2 + cs[dc]
        for dy in range(4) for dz in range(4) for dc in range(2)
    }
    peers = [(gxs[dx, dz], gys[dy, dz, dc]) for dx, dy, dz, dc in HOPS]
    sides = [(lax.rem(mx + a + NGX, NGX), lax.rem(my + b + NGY, NGY)) for a, b in SIDES]

    barrier = pltpu.get_barrier_semaphore()
    for peer in peers:
        pl.semaphore_signal(barrier, inc=1, device_id=peer, device_id_type=MESH)

    rows8 = lax.broadcasted_iota(jnp.int32, (8, TILE), 0)
    lane8 = lax.broadcasted_iota(jnp.int32, (8, TILE), 1)
    inside = rows8 < 6

    zero8 = jnp.zeros((8, TILE), F32)
    for k in range(4):
        win[k, 0:PAD] = jnp.zeros((PAD, TILE), F32)
        win[k, PAD + ROWS : FLAT] = jnp.zeros((PAD, TILE), F32)
        for ix in range(2):
            own[0, k, ix] = zero8
    for k in range(3):
        for ix in range(2):
            vel[k, ix] = zero8
            for iy in range(2):
                own[0, k, ix, 3 * iy : 3 * iy + 3] = u_in[k, ix, iy]
                vel[k, ix, 3 * iy : 3 * iy + 3] = v_in[k, ix, iy]
            for n in range(STEPS):
                kick[n, k, ix] = zero8
                for iy in range(2):
                    kick[n, k, ix, 3 * iy : 3 * iy + 3] = noise[n, k, ix, iy]
    tile_row = lax.broadcasted_iota(jnp.int32, (16, PAIRS), 0)
    slot = lax.broadcasted_iota(jnp.int32, (16, PAIRS), 1)
    tile_id = jnp.where(tile_row % 8 < 6, tile_row // 8 * 6 + tile_row % 8, -1)
    named = (pairs[0, 0, 0:1, :] == tile_id) & (slot < count[0:1, 0:1])
    coded = pairs[0, 0, 1:2, :] == lax.broadcasted_iota(jnp.int32, (TILE, PAIRS), 0)
    live = lax.dot_general(
        jnp.where(named, 1.0, 0.0).astype(jnp.bfloat16),
        jnp.where(coded, 1.0, 0.0).astype(jnp.bfloat16),
        (((1,), (1,)), ((), ())),
        preferred_element_type=F32,
    )
    own[0, 3, 0] = live[0:8]
    own[0, 3, 1] = live[8:16]
    for i in range(NGX):
        row[0, 0:1, NGY * i : NGY * (i + 1)] = heat_in[0, i : i + 1, :]

    pl.semaphore_wait(barrier, len(peers))

    def halo_copies(n, channels):
        copies = []
        for i, (a, b) in enumerate(SIDES):
            if a:
                src = own.at[n, pl.ds(0, channels), (a + 1) // 2]
                dst = arrive.at[n, i, pl.ds(0, channels), 0]
            else:
                src = own.at[n, pl.ds(0, channels)]
                dst = arrive.at[n, i, pl.ds(0, channels)]
            copies.append(
                pltpu.make_async_remote_copy(
                    src_ref=src, dst_ref=dst, send_sem=halo_send.at[n, i], recv_sem=halo_recv.at[n, i],
                    device_id=sides[i], device_id_type=MESH,
                )
            )
        return copies

    def send_all(g):
        src = row.at[g, pl.ds(0, 1)]
        dst = grid.at[g, mx, pl.ds(my, 1)]
        for peer in peers:
            pltpu.make_async_remote_copy(
                src_ref=src, dst_ref=dst, send_sem=all_send.at[g], recv_sem=all_recv.at[g],
                device_id=peer, device_id_type=MESH,
            ).start()
        pltpu.make_async_copy(src, dst, all_recv.at[g]).start()
        pltpu.make_async_copy(src, junk.at[pl.ds(0, 1)], all_send.at[g]).start()

    def wait_all(g):
        pltpu.make_async_copy(grid.at[g], grid.at[g], all_recv.at[g]).wait()
        pltpu.make_async_copy(grid.at[g], grid.at[g], all_send.at[g]).wait()

    def place(n, channel, target):
        for ix in range(2):
            start = PAD + 12 * (ix + 1) + 3
            target[start : start + 6] = own[n, channel, ix, 0:6]
        for i, (a, b) in enumerate(SIDES):
            for ix in range(2) if a == 0 else (0,):
                wx = ix + 1 if a == 0 else (0 if a == 1 else 3)
                start = PAD + 12 * wx
                if b == 0:
                    target[start + 3 : start + 9] = arrive[n, i, channel, ix, 0:6]
                elif b == 1:
                    target[start : start + 3] = arrive[n, i, channel, ix, 3:6]
                else:
                    target[start + 9 : start + 12] = arrive[n, i, channel, ix, 0:3]

    hz, cy, cx = lane8 % 8, lane8 // 8 % 4, lane8 // 32
    target_odd = (hz % 2) == 0

    def carried(cell, n):
        if n % 2 == 0:
            d = n // 2
            return cell < d if d > 0 else cell >= 4 + d
        low, high = (n - 1) // 2, (n + 1) // 2
        if n > 0:
            return (target_odd & (cell < high)) | (~target_odd & (cell < low))
        return (target_odd & (cell >= 4 + high)) | (~target_odd & (cell >= 4 + low))

    sign = lambda n: (n > 0) - (n < 0)
    carry_x = {n: carried(cx, n) for n in (-3, -2, -1, 1, 2, 3)}
    carry_y = {n: carried(cy, n) for n in (-3, -2, -1, 1, 2, 3)}
    carry_z = {n: (hz < n if n > 0 else hz >= 8 + n) for n in (-3, -2, -1, 1, 2, 3)}

    def combos(total):
        found = []
        for nx, ny, nz in OFFSETS[:total]:
            if ny and (ny, nz) not in found:
                found.append((ny, nz))
        return found

    slots = {c: i for i, c in enumerate(combos(len(OFFSETS)))}

    def stages(total, k):
        depths = sorted({nz for _, _, nz in OFFSETS[:total] if nz})
        for block in range(ROWS // 8):
            r = PAD + 8 * block
            t = (rows8 + 8 * block) % 3
            middle = win[k, r : r + 8]
            up = jnp.where(t < 2, win[k, r + 1 : r + 9], win[k, r - 2 : r + 6])
            down = jnp.where(t > 0, win[k, r - 1 : r + 7], win[k, r + 2 : r + 10])
            for nz in depths:
                zed[nz + 3, k, r : r + 8] = jnp.where(carry_z[nz], up if nz > 0 else down, middle)
            zed[3, k, r : r + 8] = middle
        for block in range(ROWS // 8):
            r = PAD + 8 * block
            for ny, nz in combos(total):
                e = r + 3 * sign(ny)
                wye[slots[ny, nz], k, r : r + 8] = jnp.where(
                    carry_y[ny], zed[nz + 3, k, e : e + 8], zed[nz + 3, k, r : r + 8]
                )

    def neighbour(o, k, r):
        nx, ny, nz = OFFSETS[o]
        get = (lambda q: wye[slots[ny, nz], k, q : q + 8]) if ny else (lambda q: zed[nz + 3, k, q : q + 8])
        here = get(r)
        if nx:
            here = jnp.where(carry_x[nx], get(r + 12 * sign(nx)), here)
        return spread(here, lanes[o])

    def pair(o, r, mine):
        nx, ny, nz = OFFSETS[o]
        delta = [
            (mine[k] - (0.5 * EDGE) * n) - neighbour(o, k, r) for k, n in enumerate((nx, ny, nz))
        ]
        square = delta[0] * delta[0] + delta[1] * delta[1] + delta[2] * delta[2]
        inverse = lax.rsqrt(square)
        return delta, square * inverse, inverse

    def step(n, total):
        for k in range(3):
            place(n, k, win.at[k])
        for k in range(3):
            stages(total, k)
        for block in range(ROWS // 8):
            r = PAD + 8 * block
            mine = [win[k, r : r + 8] for k in range(3)]
            density = zero8
            for o in range(total):
                _, distance, _ = pair(o, r, mine)
                gap = jnp.minimum(distance - RC, 0.0)
                density = density + mask[o, 8 * block : 8 * block + 8] * (gap * gap)
            win[3, r : r + 8] = -EMBED * lax.rsqrt(density)
        stages(total, 3)
        forces = []
        for ix in range(2):
            q = 15 + 12 * ix
            r = PAD + q
            mine = [win[k, r : r + 8] for k in range(3)]
            slope = win[3, r : r + 8]
            total_force = [zero8] * 3
            for o in range(total):
                delta, distance, inverse = pair(o, r, mine)
                gap = jnp.minimum(distance - RC, 0.0)
                close = jnp.minimum(distance - RP, 0.0)
                quad = (2 * C0 - RP * C1) + distance * ((3 * C1 - 2 * RP * C2) + (4 * C2) * distance)
                scalar = close * quad + (slope + neighbour(o, 3, r)) * gap
                scalar = scalar * inverse * mask[o, q : q + 8]
                total_force = [f - scalar * d for f, d in zip(total_force, delta)]
            forces.append([jnp.where(inside, f, 0.0) for f in total_force])
        return forces

    def diffuse(t):
        for _ in range(SUB):
            beside = jnp.concatenate([t[1:], t[:1]], axis=0) + jnp.concatenate([t[-1:], t[:-1]], axis=0)
            beside = beside + pltpu.roll(t, 1, 1) + pltpu.roll(t, NGY - 1, 1)
            beside = beside + pltpu.roll(t, 1, 2) + pltpu.roll(t, TILE - 1, 2)
            t = t + RATE * (beside - 6.0 * t)
        return t

    def deposit(g):
        lane3 = lax.broadcasted_iota(jnp.int32, (NGX, NGY, TILE), 2)
        added = jnp.where(lane3 == 1, 0.0, grid[g]) * (1.0 / HEAT)
        field[...] = diffuse(field[...] + added)

    def advance(n, forces):
        column = jnp.broadcast_to(field[mx, pl.ds(my, 1), :], (8, TILE))
        local = spread(column, planes[0])
        push = jnp.sqrt((2.0 * MASS / DT) * local)
        power = zero8
        largest = zero8
        for ix in range(2):
            reach = zero8
            for k in range(3):
                speed = vel[k, ix]
                speed = speed + (DT / MASS) * (forces[ix][k] - MASS * speed + push * kick[n, k, ix])
                vel[k, ix] = speed
                moved = own[n, k, ix] + DT * speed
                own[n + 1, k, ix] = moved
                reach = reach + moved * moved
                power = power + jnp.where(inside, speed * speed, 0.0)
            largest = jnp.maximum(largest, reach)
        return (MASS * DT) * power, largest

    def energies(n, power, largest):
        power = power + pltpu.roll(power, 5, 0)
        for shift in (8, 16, 32, 64):
            power = power + pltpu.roll(power, shift, 1)
        out = jnp.where(planes[2] > 0, spread(power, planes[1]), 0.0)
        out = jnp.sum(out, axis=0, keepdims=True)
        top = jnp.max(jnp.max(jnp.where(inside, largest, 0.0), axis=1, keepdims=True), axis=0, keepdims=True)
        row[n + 1, 0:1] = jnp.where(lane8[0:1] == 1, top, out)

    def full_step(n, total):
        forces = step(n, total)
        wait_all(n)

        @pl.when(n == 0)
        def _():
            field[...] = jnp.transpose(grid[0].reshape(TILE, TILE)).reshape(NGX, NGY, TILE)

        @pl.when(n > 0)
        def _():
            deposit(n)

        power, largest = advance(n, forces)

        @pl.when(n < STEPS - 1)
        def _():
            for c in halo_copies(n + 1, 3):
                c.start()

        energies(n, power, largest)
        send_all(n + 1)

        @pl.when(n < STEPS - 1)
        def _():
            for c in halo_copies(n + 1, 3):
                c.wait_recv()
            for c in halo_copies(n + 1, 3):
                c.wait_send()

    for c in halo_copies(0, 4):
        c.start()
    send_all(0)
    for c in halo_copies(0, 4):
        c.wait_recv()
    for c in halo_copies(0, 4):
        c.wait_send()

    place(0, 3, live_win)
    for block in range(ROWS // 8):
        known = live_win[PAD + 8 * block : PAD + 8 * block + 8]
        for o in range(len(OFFSETS)):
            mask[o, 8 * block : 8 * block + 8] = spread(known, lanes[len(OFFSETS) + o])

    lax.fori_loop(0, 2, lambda n, c: (full_step(n, NEAR), c)[1], 0)
    lax.fori_loop(2, 4, lambda n, c: (full_step(n, len(OFFSETS)), c)[1], 0)

    for k in range(3):
        for ix in range(2):
            for iy in range(2):
                u_out[k, ix, iy] = own[STEPS, k, ix, 3 * iy : 3 * iy + 3]
                v_out[k, ix, iy] = vel[k, ix, 3 * iy : 3 * iy + 3]
    near = jnp.max(jnp.max(grid[1], axis=0), axis=0, keepdims=True)
    far = jnp.maximum(jnp.max(grid[2], axis=0), jnp.max(grid[3], axis=0))
    far = jnp.max(far, axis=0, keepdims=True)
    flag_out[...] = jnp.where((near <= NEAR_LIMIT) & (far <= FAR_LIMIT), 1.0, 0.0)

    wait_all(STEPS)
    deposit(STEPS)
    lane3 = lax.broadcasted_iota(jnp.int32, (NGX, NGY, TILE), 2)
    heat_out[0] = jnp.sum(jnp.where(lane3 == mx * NGY + my, field[...], 0.0), axis=2)


def fast(displacement, velocity, noise, electron_temp, pair_list, pair_count):
    block = (3, 2, 2, TZ, TILE)
    whole = pl.BlockSpec(memory_space=pltpu.VMEM)
    total = len(OFFSETS)
    return pl.pallas_call(
        body,
        out_shape=(
            jax.ShapeDtypeStruct(block, F32),
            jax.ShapeDtypeStruct(block, F32),
            jax.ShapeDtypeStruct((1, NGX, NGY), F32),
            jax.ShapeDtypeStruct((1, TILE), F32),
        ),
        in_specs=[whole] * 8,
        out_specs=(whole,) * 4,
        scratch_shapes=[
            pltpu.VMEM((STEPS + 1, 4, 2, 8, TILE), F32),
            pltpu.VMEM((STEPS, 8, 4, 2, 8, TILE), F32),
            pltpu.VMEM((STEPS + 1, NGX, NGY, TILE), F32),
            pltpu.VMEM((STEPS + 1, 8, TILE), F32),
            pltpu.VMEM((4, FLAT, TILE), F32),
            pltpu.VMEM((7, 4, FLAT, TILE), F32),
            pltpu.VMEM((18, 4, FLAT, TILE), F32),
            pltpu.VMEM((total, ROWS, TILE), F32),
            pltpu.VMEM((FLAT, TILE), F32),
            pltpu.VMEM((3, 2, 8, TILE), F32),
            pltpu.VMEM((STEPS, 3, 2, 8, TILE), F32),
            pltpu.VMEM((NGX, NGY, TILE), F32),
            pltpu.SemaphoreType.DMA((STEPS, 8)),
            pltpu.SemaphoreType.DMA((STEPS, 8)),
            pltpu.SemaphoreType.DMA((STEPS + 1,)),
            pltpu.SemaphoreType.DMA((STEPS + 1,)),
            pltpu.VMEM((8, TILE), F32),
        ],
        compiler_params=pltpu.CompilerParams(
            collective_id=0, has_side_effects=True, vmem_limit_bytes=40 << 20
        ),
    )(
        displacement, velocity, noise, electron_temp, pair_list, pair_count,
        jnp.asarray(lane_tables()), jnp.asarray(plane_tables()),
    )


def padded_2(values, sides, width):
    for axis, dim in sides:
        count = lax.axis_size(axis)
        forward = [(i, (i + 1) % count) for i in range(count)]
        backward = [(target, source) for source, target in forward]
        low = lax.ppermute(lax.slice_in_dim(values, values.shape[dim] - width, None, axis=dim), axis, forward)
        high = lax.ppermute(lax.slice_in_dim(values, 0, width, axis=dim), axis, backward)
        values = jnp.concatenate([low, values, high], axis=dim)
    return values


def lattice_sites():
    serial = jnp.arange(TILE, dtype=jnp.int32)
    cell = serial // 2
    corners = jnp.stack([cell // 16, cell // 4 % 4, cell % 4])
    return EDGE * (corners.astype(F32) + ((serial % 2).astype(F32) * 0.5)[None, :])


def pair_geometry(flat, tile_index, code, lattice):
    t, iy, ix = tile_index % TZ, tile_index // TZ % 2, tile_index // (TZ * 2)
    ex, ey, ez = code // 9, code // 3 % 3, code % 3
    own_index = ((ix + 1) * 4 + iy + 1) * TZ + t
    other_index = ((ix + ex) * 4 + iy + ey) * TZ + (t + ez - 1 + TZ) % TZ
    own_tile = lax.dynamic_index_in_dim(flat, own_index, 1, keepdims=False)
    other_tile = lax.dynamic_index_in_dim(flat, other_index, 1, keepdims=False)
    offset = jnp.stack([ex - 1, ey - 1, ez - 1]).astype(F32) * (4 * EDGE)
    delta = (lattice + own_tile)[:, :, None] - (lattice + other_tile + offset[:, None])[:, None, :]
    square = jnp.sum(delta * delta, axis=0)
    serial = jnp.arange(TILE, dtype=jnp.int32)
    same = (code == 13) & (serial[:, None] == serial[None, :])
    return delta, jnp.sqrt(jnp.where(same, 100.0, square)), own_index, other_index


def density_term(flat, lattice, tile_index, code):
    _, distance, _, _ = pair_geometry(flat, tile_index, code, lattice)
    gap = distance - RC
    return jnp.sum(jnp.where(distance < RC, gap * gap, 0.0), axis=1)[None]


def force_term(flat, embed, lattice, tile_index, code):
    delta, distance, own_index, other_index = pair_geometry(flat, tile_index, code, lattice)
    own_embed = lax.dynamic_index_in_dim(embed, own_index, 0, keepdims=False)
    other_embed = lax.dynamic_index_in_dim(embed, other_index, 0, keepdims=False)
    gap = distance - RP
    poly = C0 + C1 * distance + C2 * distance * distance
    slope = jnp.where(distance < RP, 2.0 * gap * poly + gap * gap * (C1 + 2.0 * C2 * distance), 0.0)
    dens = jnp.where(distance < RC, 2.0 * (distance - RC), 0.0)
    scalar = (slope + (own_embed[:, None] + other_embed[None, :]) * dens) / distance
    return -jnp.sum(scalar[None] * delta, axis=2)


def sweep(term, channels, table, total):
    def visit(i, running):
        entry = lax.dynamic_slice_in_dim(table, i, 1, 1)
        u = entry[0, 0]
        value = jnp.where(i < total, term(u, entry[1, 0]), 0.0)
        old = lax.dynamic_slice_in_dim(running, u, 1, 1)
        return lax.dynamic_update_slice_in_dim(running, old + value[:, None], u, 1)

    running = lax.fori_loop(0, PAIRS, visit, jnp.zeros((channels, TILES, TILE), F32))
    return running.reshape(channels, 2, 2, TZ, TILE)


def slow(displacement, velocity, noise, electron_temp, pair_list, pair_count):
    lattice = lattice_sites()
    table, total = pair_list[0, 0], pair_count[0, 0]
    owners = NGX * NGY
    serial = np.arange(TZ * TILE)
    layer = serial // TILE * 8 + serial % 8
    onehot = jnp.asarray((layer * owners // 24)[:, None] == np.arange(owners)[None, :])
    axes = (("gx", 1), ("gy", 2))

    def one(n, carry):
        positions, speeds, heat = carry
        arrived = lax.all_to_all(heat.reshape(1, owners), ("gx", "gy"), split_axis=1, concat_axis=0, tiled=True)
        local = jnp.sum(jnp.where(onehot, arrived.reshape(1, owners), 0.0), axis=1).reshape(1, 1, 1, TZ, TILE)
        flat = padded_2(positions, axes, 1).reshape(3, 16 * TZ, TILE)
        density = sweep(partial(density_term, flat, lattice), 1, table, total)
        embed = padded_2(-EMBED / (2.0 * jnp.sqrt(density)), axes, 1).reshape(16 * TZ, TILE)
        force = sweep(partial(force_term, flat, embed, lattice), 3, table, total)
        kicker = jnp.sqrt(2.0 * MASS * local / DT) * lax.dynamic_index_in_dim(noise, n, 0, keepdims=False)
        speeds = speeds + DT / MASS * (force - MASS * speeds + kicker)
        positions = positions + DT * speeds
        power = MASS * DT * jnp.sum(speeds * speeds, axis=0)
        power = jnp.sum(power, axis=(0, 1)).reshape(-1, 1)
        energy = jnp.sum(jnp.where(onehot, power, 0.0), axis=0)
        arrived = lax.all_to_all(energy.reshape(owners, 1), ("gx", "gy"), split_axis=0, concat_axis=1, tiled=True)
        heat = heat + arrived.reshape(1, NGX, NGY) / HEAT

        def relax(_, heat):
            padded = padded_2(heat, ((("gx", "gy"), 0),), 1)
            beside = padded[2:] + padded[:-2] + jnp.roll(heat, 1, 1) + jnp.roll(heat, -1, 1)
            beside = beside + jnp.roll(heat, 1, 2) + jnp.roll(heat, -1, 2)
            return heat + RATE * (beside - 6.0 * heat)

        return positions, speeds, lax.fori_loop(0, SUB, relax, heat)

    return lax.fori_loop(0, STEPS, one, (displacement, velocity, electron_temp))


def per_device(*arguments):
    *results, flag = fast(*arguments)
    return lax.cond(flag[0, 1] > 0.5, lambda: tuple(results), lambda: slow(*arguments))


def solution(mesh):
    brick = P(None, "gx", "gy", None, None)
    placed = (
        brick,
        brick,
        P(None, None, "gx", "gy", None, None),
        P(("gx", "gy"), None, None),
        P("gx", "gy", None, None),
        P("gx", "gy"),
    )
    return jax.shard_map(
        per_device, mesh=mesh, in_specs=placed, out_specs=(brick, brick, P(("gx", "gy"), None, None)), check_vma=False
    )
```

```python
from functools import partial

import jax
import jax.numpy as jnp
import numpy as np
from jax import lax
from jax.experimental import pallas as pl
from jax.experimental.pallas import tpu as pltpu
from jax.sharding import PartitionSpec as P

MESH = pl.DeviceIdType.MESH
NGX, NGY = 8, 16
TZ, TILE, TILES, STEPS, SUB = 3, 128, 12, 4, 6
PAIRS = 324

EDGE = 3.1652
RC = 4.400224
EMBED = 1.896373
RP = 3.25
C0, C1, C2 = 47.1346499, -33.7665655, 6.2541999
DT = 0.005
MASS = 0.0190534
HEAT = 0.02
RATE = 0.12

F32 = jnp.float32
OWN = 24
PAD = 16
ROWS = 48
FLAT = PAD + ROWS + PAD
FIRST, BLOCKS = 6, 5

OFFSETS = sorted(
    (
        (nx, ny, nz)
        for nx in range(-3, 4)
        for ny in range(-3, 4)
        for nz in range(-3, 4)
        if nx % 2 == ny % 2 == nz % 2 and 0 < nx * nx + ny * ny + nz * nz <= 12
    ),
    key=lambda n: (n[0] ** 2 + n[1] ** 2 + n[2] ** 2 > 8, n[1], n[2], n[0]),
)
NEAR = 26
NEAR_LIMIT = 0.42**2
FAR_LIMIT = 0.96**2


def combos(total):
    found = []
    for _, ny, nz in OFFSETS[:total]:
        if (ny, nz) != (0, 0) and (ny, nz) not in found:
            found.append((ny, nz))
    return found


SHIFTS = combos(len(OFFSETS))
SLOT = {c: i for i, c in enumerate(SHIFTS)}
SLOT[0, 0] = len(SHIFTS)
SIDES = [(a, b) for a in (-1, 0, 1) for b in (-1, 0, 1) if (a, b) != (0, 0)]
HOPS = sorted(
    (
        (dx, dy, dz, dc)
        for dx in range(4)
        for dy in range(4)
        for dz in range(4)
        for dc in range(2)
        if (dx, dy, dz, dc) != (0, 0, 0, 0)
    ),
    key=lambda d: -sum(min(v, 4 - v) for v in d[:3]) * 2 - d[3],
)
SOURCE, CODE, PLANE, BACK, HELD = 0, 20, 41, 44, 45


def lane_tables():
    s = np.arange(TILE)
    cell, hz = s // 8, s % 8
    out = []
    for ny, nz in SHIFTS:
        dy = (ny - ny % 2) // 2 + ny % 2 * (hz % 2)
        out.append((cell + dy) % 16 * 8 + (hz + nz) % 8)
    for ny, nz in SHIFTS + [(0, 0)]:
        dy = (ny - ny % 2) // 2 + ny % 2 * (hz % 2)
        out.append(s // 32 * 32 + 9 + 3 * ((cell % 4 + dy) // 4 + 1) + (hz + nz) // 8 + 1)
    out = [np.broadcast_to(v[None, :], (8, TILE)) for v in out]
    rows = np.arange(OWN)[:, None] % 3
    out += list(((rows * 8 + hz[None, :]) * 128 // 24).reshape(3, 8, TILE))
    back, held = np.zeros((8, TILE)), np.zeros((OWN, TILE))
    for layer in range(24):
        back[:, layer * 128 // 24] = layer % 8
        held[:, layer * 128 // 24] = rows[:, 0] == layer // 8
    out += [back] + list(held.reshape(3, 8, TILE))
    return np.stack(out).astype(np.int32)


def spread(x, index):
    return jnp.take_along_axis(x, index, axis=1, mode="promise_in_bounds")


def body(
    u_in, v_in, noise, heat_in, pairs_in, count, tables,
    u_out, v_out, heat_out, flag_out,
    own, turned, arrive, grid, row, win, shifted, mask, live_win, vel, kick, field,
    raw, back, heat, pairs, lanes,
    in_sem, halo_send, halo_recv, all_send, all_recv, junk,
):
    mx, my = lax.axis_index("gx"), lax.axis_index("gy")
    x, zl = lax.rem(mx, 4), mx // 4
    y, zh, core = my // 4, lax.rem(my // 2, 2), lax.rem(my, 2)
    z = zh * 2 + zl
    xs = [lax.rem(x + d, 4) for d in range(4)]
    ys = [lax.rem(y + d, 4) for d in range(4)]
    zs = [lax.rem(z + d, 4) for d in range(4)]
    cs = [lax.rem(core + d, 2) for d in range(2)]
    gxs = {(dx, dz): lax.rem(zs[dz], 2) * 4 + xs[dx] for dx in range(4) for dz in range(4)}
    gys = {
        (dy, dz, dc): ys[dy] * 4 + zs[dz] // 2 * 2 + cs[dc]
        for dy in range(4) for dz in range(4) for dc in range(2)
    }
    peers = [(gxs[dx, dz], gys[dy, dz, dc]) for dx, dy, dz, dc in HOPS]
    sides = [(lax.rem(mx + a + NGX, NGX), lax.rem(my + b + NGY, NGY)) for a, b in SIDES]

    barrier = pltpu.get_barrier_semaphore()
    for peer in peers:
        pl.semaphore_signal(barrier, inc=1, device_id=peer, device_id_type=MESH)

    loads = [
        pltpu.make_async_copy(pairs_in, pairs, in_sem.at[0]),
        pltpu.make_async_copy(heat_in, heat, in_sem.at[1]),
        pltpu.make_async_copy(tables, lanes, in_sem.at[2]),
    ]
    for ix in range(2):
        for iy in range(2):
            spot = pl.ds(3 * ix, 3)
            at = 3 + 3 * (2 * ix + iy)
            loads += [
                pltpu.make_async_copy(u_in.at[:, ix, :, iy], raw.at[iy, pl.ds(0, 3), spot], in_sem.at[at]),
                pltpu.make_async_copy(v_in.at[:, ix, :, iy], raw.at[iy, pl.ds(3, 3), spot], in_sem.at[at + 1]),
            ] + [
                pltpu.make_async_copy(
                    noise.at[n, :, ix, :, iy], raw.at[iy, pl.ds(6 + 3 * n, 3), spot], in_sem.at[15 + 4 * n + 2 * ix + iy]
                )
                for n in range(STEPS)
            ]
    for copy in loads:
        copy.start()

    rows8 = lax.broadcasted_iota(jnp.int32, (8, TILE), 0)
    lane8 = lax.broadcasted_iota(jnp.int32, (8, TILE), 1)
    hz = lane8 % 8
    odd = hz % 2 == 1
    inside = (lane8 >= 32) & (lane8 < 96)
    zero8 = jnp.zeros((8, TILE), F32)

    for k in range(4):
        win[k] = jnp.zeros((FLAT, TILE), F32)
    live_win[...] = jnp.zeros((FLAT, TILE), F32)
    for i in range(len(SHIFTS)):
        for k in range(4):
            shifted[i, k, 0:PAD] = jnp.zeros((PAD, TILE), F32)
            shifted[i, k, PAD + ROWS : FLAT] = jnp.zeros((PAD, TILE), F32)

    for copy in loads:
        copy.wait()

    def gathered(c, cell):
        low, high = raw[0, c], raw[1, c]
        low = low if cell == 1 else pltpu.roll(low, (32 * (1 - cell)) % TILE, 1)
        high = high if cell == 2 else pltpu.roll(high, (32 * (2 - cell)) % TILE, 1)
        return jnp.where(lane8 < 64, low, high)

    def unpack(c, target):
        for cell in range(4):
            value = jnp.where(inside, gathered(c, cell), 0.0)
            for ix in range(2):
                start = (4 * ix + cell) * 3
                target[start : start + 3] = value[3 * ix : 3 * ix + 3]

    for k in range(3):
        unpack(k, own.at[0, k])
        unpack(3 + k, vel.at[k])

    p_row = lax.broadcasted_iota(jnp.int32, (OWN, PAIRS), 0)
    p_lane = lax.broadcasted_iota(jnp.int32, (TILE, PAIRS), 0)
    slot = lax.broadcasted_iota(jnp.int32, (OWN, PAIRS), 1)
    tile, code = pairs[0, 0, 0:1, :], pairs[0, 0, 1:2, :]
    named = (tile // 6 * 3 + tile % 3 == p_row // 12 * 3 + p_row % 3) & (slot < count[0:1, 0:1])
    coded = tile // 3 % 2 * 32 + 32 + code == p_lane
    own[0, 3] = lax.dot_general(
        jnp.where(named, 1.0, 0.0).astype(jnp.bfloat16),
        jnp.where(coded, 1.0, 0.0).astype(jnp.bfloat16),
        (((1,), (1,)), ((), ())),
        preferred_element_type=F32,
    )
    for k in range(4):
        turned[0, k] = pltpu.roll(own[0, k], 64, 1)
    for i in range(NGX):
        row[0, 0:1, NGY * i : NGY * (i + 1)] = heat[0, i : i + 1, :]

    pl.semaphore_wait(barrier, len(peers))

    def halo_copies(n, channels):
        copies = []
        for i, (a, b) in enumerate(SIDES):
            source = turned if b else own
            if a:
                src = source.at[n, pl.ds(0, channels), pl.ds(12 if a > 0 else 0, 12)]
                dst = arrive.at[n, i, pl.ds(0, channels), pl.ds(0, 12)]
            else:
                src = source.at[n, pl.ds(0, channels)]
                dst = arrive.at[n, i, pl.ds(0, channels)]
            copies.append(
                pltpu.make_async_remote_copy(
                    src_ref=src, dst_ref=dst, send_sem=halo_send.at[n, i], recv_sem=halo_recv.at[n, i],
                    device_id=sides[i], device_id_type=MESH,
                )
            )
        return copies

    def send_all(g):
        src = row.at[g, pl.ds(0, 1)]
        dst = grid.at[g, mx, pl.ds(my, 1)]
        for peer in peers:
            pltpu.make_async_remote_copy(
                src_ref=src, dst_ref=dst, send_sem=all_send.at[g], recv_sem=all_recv.at[g],
                device_id=peer, device_id_type=MESH,
            ).start()
        pltpu.make_async_copy(src, dst, all_recv.at[g]).start()
        pltpu.make_async_copy(src, junk.at[pl.ds(0, 1)], all_send.at[g]).start()

    def wait_all(g):
        pltpu.make_async_copy(grid.at[g], grid.at[g], all_recv.at[g]).wait()
        pltpu.make_async_copy(grid.at[g], grid.at[g], all_send.at[g]).wait()

    def place(n, channel, target):
        for start, size, a in ((0, 12, 1), (12, 24, 0), (36, 12, -1)):
            low = arrive[n, SIDES.index((a, 1)), channel, 0:size]
            high = arrive[n, SIDES.index((a, -1)), channel, 0:size]
            middle = arrive[n, SIDES.index((a, 0)), channel, 0:size] if a else own[n, channel]
            lane = lax.broadcasted_iota(jnp.int32, (size, TILE), 1)
            target[PAD + start : PAD + start + size] = jnp.where(
                lane < 32, low, jnp.where(lane < 96, middle, high)
            )

    carry = {n: (hz < n if n > 0 else hz >= 8 + n) for n in (-3, -2, -1, 1, 2, 3)}

    def stage(total, k):
        wanted = combos(total)
        for block in range(ROWS // 8):
            r = PAD + 8 * block
            t = (rows8 + 8 * block) % 3
            middle = win[k, r : r + 8]
            up = jnp.where(t < 2, win[k, r + 1 : r + 9], win[k, r - 2 : r + 6])
            down = jnp.where(t > 0, win[k, r - 1 : r + 7], win[k, r + 2 : r + 10])
            for depth in sorted({nz for _, nz in wanted}):
                source = jnp.where(carry[depth], up if depth > 0 else down, middle) if depth else middle
                for ny, nz in wanted:
                    if nz == depth:
                        i = SLOT[ny, nz]
                        shifted[i, k, r : r + 8] = spread(source, lanes[SOURCE + i])

    def neighbour(o, k, r):
        nx, ny, nz = OFFSETS[o]
        i = SLOT[ny, nz]
        get = (lambda q: shifted[i, k, q : q + 8]) if (ny, nz) != (0, 0) else (lambda q: win[k, q : q + 8])
        if nx % 2 == 0:
            return get(r + 3 * (nx // 2))
        return jnp.where(odd, get(r + 3 * ((nx + 1) // 2)), get(r + 3 * ((nx - 1) // 2)))

    def pair(o, r, mine):
        delta = [
            (mine[k] - (0.5 * EDGE) * n) - neighbour(o, k, r) for k, n in enumerate(OFFSETS[o])
        ]
        square = delta[0] * delta[0] + delta[1] * delta[1] + delta[2] * delta[2]
        inverse = lax.rsqrt(square)
        return delta, square * inverse, inverse

    def masks(first, last):
        for block in range(BLOCKS):
            start = FIRST + 8 * block
            cell = (rows8 + start) // 3 % 4
            known = live_win[PAD + start : PAD + start + 8]
            over = {}
            for nx in range(-3, 4):
                dx = cell + (nx // 2 if nx % 2 == 0 else (nx - 1) // 2 + hz % 2)
                over[nx] = jnp.where(dx > 3, 9, jnp.where(dx < 0, -9, 0))
            for o in range(first, last):
                nx, ny, nz = OFFSETS[o]
                mask[o, 8 * block : 8 * block + 8] = spread(known, lanes[CODE + SLOT[ny, nz]] + over[nx])

    def step(n, total):
        for k in range(3):
            place(n, k, win.at[k])
        for k in range(3):
            stage(total, k)
        for block in range(BLOCKS):
            r = PAD + FIRST + 8 * block
            mine = [win[k, r : r + 8] for k in range(3)]
            density = zero8
            for o in range(total):
                _, distance, _ = pair(o, r, mine)
                gap = jnp.minimum(distance - RC, 0.0)
                density = density + mask[o, 8 * block : 8 * block + 8] * (gap * gap)
            win[3, r : r + 8] = -EMBED * lax.rsqrt(density)
        stage(total, 3)
        forces = []
        for block in range(OWN // 8):
            r = PAD + 12 + 8 * block
            q = 12 - FIRST + 8 * block
            mine = [win[k, r : r + 8] for k in range(3)]
            slope = win[3, r : r + 8]
            total_force = [zero8] * 3
            for o in range(total):
                delta, distance, inverse = pair(o, r, mine)
                gap = jnp.minimum(distance - RC, 0.0)
                close = jnp.minimum(distance - RP, 0.0)
                quad = (2 * C0 - RP * C1) + distance * ((3 * C1 - 2 * RP * C2) + (4 * C2) * distance)
                scalar = close * quad + (slope + neighbour(o, 3, r)) * gap
                scalar = scalar * inverse * mask[o, q : q + 8]
                total_force = [f - scalar * d for f, d in zip(total_force, delta)]
            forces.append([jnp.where(inside, f, 0.0) for f in total_force])
        return forces

    def diffuse(t):
        for _ in range(SUB):
            beside = jnp.concatenate([t[1:], t[:1]], axis=0) + jnp.concatenate([t[-1:], t[:-1]], axis=0)
            beside = beside + pltpu.roll(t, 1, 1) + pltpu.roll(t, NGY - 1, 1)
            beside = beside + pltpu.roll(t, 1, 2) + pltpu.roll(t, TILE - 1, 2)
            t = t + RATE * (beside - 6.0 * t)
        return t

    def deposit(g):
        lane3 = lax.broadcasted_iota(jnp.int32, (NGX, NGY, TILE), 2)
        added = jnp.where(lane3 == 1, 0.0, grid[g]) * (1.0 / HEAT)
        field[...] = diffuse(field[...] + added)

    def advance(n, forces):
        column = jnp.broadcast_to(field[mx, pl.ds(my, 1), :], (8, TILE))
        power, largest = [], zero8
        for block in range(OWN // 8):
            at = slice(8 * block, 8 * block + 8)
            push = jnp.sqrt((2.0 * MASS / DT) * spread(column, lanes[PLANE + block]))
            reach = zero8
            energy = zero8
            for k in range(3):
                speed = vel[k, at]
                speed = speed + (DT / MASS) * (forces[block][k] - MASS * speed + push * kick[n, k, at])
                vel[k, at] = speed
                moved = win[k, PAD + 12 + 8 * block : PAD + 20 + 8 * block] + DT * speed
                own[n + 1, k, at] = moved
                turned[n + 1, k, at] = pltpu.roll(moved, 64, 1)
                reach = reach + moved * moved
                energy = energy + speed * speed
            largest = jnp.maximum(largest, reach)
            power.append(energy)
        return power, largest

    def energies(n, power, largest):
        out = zero8
        for block in range(OWN // 8):
            value = power[block]
            for shift in (8, 16, 32, 64):
                value = value + pltpu.roll(value, shift, 1)
            out = out + jnp.where(lanes[HELD + block] > 0, spread(value, lanes[BACK]), 0.0)
        out = (MASS * DT) * jnp.sum(out, axis=0, keepdims=True)
        top = jnp.max(jnp.max(jnp.where(inside, largest, 0.0), axis=1, keepdims=True), axis=0, keepdims=True)
        row[n + 1, 0:1] = jnp.where(lane8[0:1] == 1, top, out)

    def full_step(n, total):
        forces = step(n, total)
        wait_all(n)

        @pl.when(n == 0)
        def _():
            field[...] = jnp.transpose(grid[0].reshape(TILE, TILE)).reshape(NGX, NGY, TILE)

        @pl.when(n > 0)
        def _():
            deposit(n)

        power, largest = advance(n, forces)

        @pl.when(n < STEPS - 1)
        def _():
            for c in halo_copies(n + 1, 3):
                c.start()

        energies(n, power, largest)
        send_all(n + 1)

        @pl.when(n == 0)
        def _():
            masks(NEAR, len(OFFSETS))

        @pl.when(n < STEPS - 1)
        def _():
            waits = halo_copies(n + 1, 3)
            for c in waits:
                c.wait_recv()
            for c in waits:
                c.wait_send()

    first = halo_copies(0, 4)
    for c in first:
        c.start()
    send_all(0)
    for n in range(STEPS):
        for k in range(3):
            unpack(6 + 3 * n + k, kick.at[n, k])
    for c in first:
        c.wait_recv()
    for c in first:
        c.wait_send()

    place(0, 3, live_win)
    masks(0, NEAR)

    lax.fori_loop(0, 2, lambda n, c: (full_step(n, NEAR), c)[1], 0)
    lax.fori_loop(2, 4, lambda n, c: (full_step(n, len(OFFSETS)), c)[1], 0)

    for c in range(6):
        held = own.at[STEPS, c] if c < 3 else vel.at[c - 3]
        for cell in range(4):
            for ix in range(2):
                start = (4 * ix + cell) * 3
                raw[0, cell, 3 * ix : 3 * ix + 3] = held[start : start + 3]
        for iy in range(2):
            value = zero8
            for cell in range(4):
                part = raw[0, cell]
                part = part if cell == 1 + iy else pltpu.roll(part, (32 * (cell - 1 - iy)) % TILE, 1)
                value = jnp.where(lane8 // 32 == cell, part, value)
            back[iy, c] = value
    stores = []
    for ix in range(2):
        for iy in range(2):
            spot = pl.ds(3 * ix, 3)
            at = 3 + 3 * (2 * ix + iy)
            stores += [
                pltpu.make_async_copy(back.at[iy, pl.ds(0, 3), spot], u_out.at[:, ix, :, iy], in_sem.at[at]),
                pltpu.make_async_copy(back.at[iy, pl.ds(3, 3), spot], v_out.at[:, ix, :, iy], in_sem.at[at + 1]),
            ]
    for copy in stores:
        copy.start()
    lane1 = lane8[0:1] == 1
    near = jnp.max(jnp.max(grid[1], axis=0), axis=0, keepdims=True)
    far = jnp.maximum(jnp.max(grid[2], axis=0), jnp.max(grid[3], axis=0))
    far = jnp.max(far, axis=0, keepdims=True)
    fine = jnp.where((near <= NEAR_LIMIT) & (far <= FAR_LIMIT), 1.0, 0.0)
    flag_out[0, 0] = jnp.sum(jnp.where(lane1, fine, 0.0))

    wait_all(STEPS)
    deposit(STEPS)
    lane3 = lax.broadcasted_iota(jnp.int32, (NGX, NGY, TILE), 2)
    heat_out[0] = jnp.sum(jnp.where(lane3 == mx * NGY + my, field[...], 0.0), axis=2)
    for copy in stores:
        copy.wait()


def fast(displacement, velocity, noise, electron_temp, pair_list, pair_count):
    turn = lambda v: jnp.swapaxes(v, -3, -2)
    brick = (3, 2, TZ, 2, TILE)
    hbm = pl.BlockSpec(memory_space=pltpu.HBM)
    vmem = pl.BlockSpec(memory_space=pltpu.VMEM)
    total = len(OFFSETS)
    tables = lane_tables()
    u, v, heat, flag = pl.pallas_call(
        body,
        out_shape=(
            jax.ShapeDtypeStruct(brick, F32),
            jax.ShapeDtypeStruct(brick, F32),
            jax.ShapeDtypeStruct((1, NGX, NGY), F32),
            jax.ShapeDtypeStruct((1, 1), F32),
        ),
        in_specs=[hbm] * 5 + [vmem, hbm],
        out_specs=(hbm, hbm, vmem, pl.BlockSpec(memory_space=pltpu.SMEM)),
        scratch_shapes=[
            pltpu.VMEM((STEPS + 1, 4, OWN, TILE), F32),
            pltpu.VMEM((STEPS + 1, 4, OWN, TILE), F32),
            pltpu.VMEM((STEPS, 8, 4, OWN, TILE), F32),
            pltpu.VMEM((STEPS + 1, NGX, NGY, TILE), F32),
            pltpu.VMEM((STEPS + 1, 8, TILE), F32),
            pltpu.VMEM((4, FLAT, TILE), F32),
            pltpu.VMEM((len(SHIFTS), 4, FLAT, TILE), F32),
            pltpu.VMEM((total, 8 * BLOCKS, TILE), F32),
            pltpu.VMEM((FLAT, TILE), F32),
            pltpu.VMEM((3, OWN, TILE), F32),
            pltpu.VMEM((STEPS, 3, OWN, TILE), F32),
            pltpu.VMEM((NGX, NGY, TILE), F32),
            pltpu.VMEM((2, 18, 8, TILE), F32),
            pltpu.VMEM((2, 6, 8, TILE), F32),
            pltpu.VMEM((1, NGX, NGY), F32),
            pltpu.VMEM((1, 1, 2, PAIRS), jnp.int32),
            pltpu.VMEM(tables.shape, jnp.int32),
            pltpu.SemaphoreType.DMA((15 + 4 * STEPS,)),
            pltpu.SemaphoreType.DMA((STEPS, 8)),
            pltpu.SemaphoreType.DMA((STEPS, 8)),
            pltpu.SemaphoreType.DMA((STEPS + 1,)),
            pltpu.SemaphoreType.DMA((STEPS + 1,)),
            pltpu.VMEM((8, TILE), F32),
        ],
        compiler_params=pltpu.CompilerParams(
            collective_id=0, has_side_effects=True, vmem_limit_bytes=40 << 20
        ),
    )(turn(displacement), turn(velocity), turn(noise), electron_temp, pair_list, pair_count, jnp.asarray(tables))
    return turn(u), turn(v), heat, flag


def padded_2(values, sides, width):
    for axis, dim in sides:
        count = lax.axis_size(axis)
        forward = [(i, (i + 1) % count) for i in range(count)]
        backward = [(target, source) for source, target in forward]
        low = lax.ppermute(lax.slice_in_dim(values, values.shape[dim] - width, None, axis=dim), axis, forward)
        high = lax.ppermute(lax.slice_in_dim(values, 0, width, axis=dim), axis, backward)
        values = jnp.concatenate([low, values, high], axis=dim)
    return values


def lattice_sites():
    serial = jnp.arange(TILE, dtype=jnp.int32)
    cell = serial // 2
    corners = jnp.stack([cell // 16, cell // 4 % 4, cell % 4])
    return EDGE * (corners.astype(F32) + ((serial % 2).astype(F32) * 0.5)[None, :])


def pair_geometry(flat, tile_index, code, lattice):
    t, iy, ix = tile_index % TZ, tile_index // TZ % 2, tile_index // (TZ * 2)
    ex, ey, ez = code // 9, code // 3 % 3, code % 3
    own_index = ((ix + 1) * 4 + iy + 1) * TZ + t
    other_index = ((ix + ex) * 4 + iy + ey) * TZ + (t + ez - 1 + TZ) % TZ
    own_tile = lax.dynamic_index_in_dim(flat, own_index, 1, keepdims=False)
    other_tile = lax.dynamic_index_in_dim(flat, other_index, 1, keepdims=False)
    offset = jnp.stack([ex - 1, ey - 1, ez - 1]).astype(F32) * (4 * EDGE)
    delta = (lattice + own_tile)[:, :, None] - (lattice + other_tile + offset[:, None])[:, None, :]
    square = jnp.sum(delta * delta, axis=0)
    serial = jnp.arange(TILE, dtype=jnp.int32)
    same = (code == 13) & (serial[:, None] == serial[None, :])
    return delta, jnp.sqrt(jnp.where(same, 100.0, square)), own_index, other_index


def density_term(flat, lattice, tile_index, code):
    _, distance, _, _ = pair_geometry(flat, tile_index, code, lattice)
    gap = distance - RC
    return jnp.sum(jnp.where(distance < RC, gap * gap, 0.0), axis=1)[None]


def force_term(flat, embed, lattice, tile_index, code):
    delta, distance, own_index, other_index = pair_geometry(flat, tile_index, code, lattice)
    own_embed = lax.dynamic_index_in_dim(embed, own_index, 0, keepdims=False)
    other_embed = lax.dynamic_index_in_dim(embed, other_index, 0, keepdims=False)
    gap = distance - RP
    poly = C0 + C1 * distance + C2 * distance * distance
    slope = jnp.where(distance < RP, 2.0 * gap * poly + gap * gap * (C1 + 2.0 * C2 * distance), 0.0)
    dens = jnp.where(distance < RC, 2.0 * (distance - RC), 0.0)
    scalar = (slope + (own_embed[:, None] + other_embed[None, :]) * dens) / distance
    return -jnp.sum(scalar[None] * delta, axis=2)


def sweep(term, channels, table, total):
    def visit(i, running):
        entry = lax.dynamic_slice_in_dim(table, i, 1, 1)
        u = entry[0, 0]
        value = jnp.where(i < total, term(u, entry[1, 0]), 0.0)
        old = lax.dynamic_slice_in_dim(running, u, 1, 1)
        return lax.dynamic_update_slice_in_dim(running, old + value[:, None], u, 1)

    running = lax.fori_loop(0, PAIRS, visit, jnp.zeros((channels, TILES, TILE), F32))
    return running.reshape(channels, 2, 2, TZ, TILE)


def slow(displacement, velocity, noise, electron_temp, pair_list, pair_count):
    lattice = lattice_sites()
    table, total = pair_list[0, 0], pair_count[0, 0]
    owners = NGX * NGY
    serial = np.arange(TZ * TILE)
    layer = serial // TILE * 8 + serial % 8
    onehot = jnp.asarray((layer * owners // 24)[:, None] == np.arange(owners)[None, :])
    axes = (("gx", 1), ("gy", 2))

    def one(n, carry):
        positions, speeds, heat = carry
        arrived = lax.all_to_all(heat.reshape(1, owners), ("gx", "gy"), split_axis=1, concat_axis=0, tiled=True)
        local = jnp.sum(jnp.where(onehot, arrived.reshape(1, owners), 0.0), axis=1).reshape(1, 1, 1, TZ, TILE)
        flat = padded_2(positions, axes, 1).reshape(3, 16 * TZ, TILE)
        density = sweep(partial(density_term, flat, lattice), 1, table, total)
        embed = padded_2(-EMBED / (2.0 * jnp.sqrt(density)), axes, 1).reshape(16 * TZ, TILE)
        force = sweep(partial(force_term, flat, embed, lattice), 3, table, total)
        kicker = jnp.sqrt(2.0 * MASS * local / DT) * lax.dynamic_index_in_dim(noise, n, 0, keepdims=False)
        speeds = speeds + DT / MASS * (force - MASS * speeds + kicker)
        positions = positions + DT * speeds
        power = MASS * DT * jnp.sum(speeds * speeds, axis=0)
        power = jnp.sum(power, axis=(0, 1)).reshape(-1, 1)
        energy = jnp.sum(jnp.where(onehot, power, 0.0), axis=0)
        arrived = lax.all_to_all(energy.reshape(owners, 1), ("gx", "gy"), split_axis=0, concat_axis=1, tiled=True)
        heat = heat + arrived.reshape(1, NGX, NGY) / HEAT

        def relax(_, heat):
            padded = padded_2(heat, ((("gx", "gy"), 0),), 1)
            beside = padded[2:] + padded[:-2] + jnp.roll(heat, 1, 1) + jnp.roll(heat, -1, 1)
            beside = beside + jnp.roll(heat, 1, 2) + jnp.roll(heat, -1, 2)
            return heat + RATE * (beside - 6.0 * heat)

        return positions, speeds, lax.fori_loop(0, SUB, relax, heat)

    return lax.fori_loop(0, STEPS, one, (displacement, velocity, electron_temp))


def per_device(*arguments):
    *results, flag = fast(*arguments)
    return lax.cond(flag[0, 0] > 0.5, lambda: tuple(results), lambda: slow(*arguments))


def solution(mesh):
    brick = P(None, "gx", "gy", None, None)
    placed = (
        brick,
        brick,
        P(None, None, "gx", "gy", None, None),
        P(("gx", "gy"), None, None),
        P("gx", "gy", None, None),
        P("gx", "gy"),
    )
    return jax.shard_map(
        per_device, mesh=mesh, in_specs=placed, out_specs=(brick, brick, P(("gx", "gy"), None, None)), check_vma=False
    )
```

```python
import math
from functools import partial

import jax
import jax.numpy as jnp
import numpy as np
from jax import lax
from jax.experimental import pallas as pl
from jax.experimental.pallas import tpu as pltpu
from jax.sharding import PartitionSpec as P

MESH = pl.DeviceIdType.MESH
NGX, NGY = 8, 16
TZ, TILE, TILES, STEPS, SUB = 3, 128, 12, 4, 6
PAIRS = 324

EDGE = 3.1652
RC = 4.400224
EMBED = 1.896373
RP = 3.25
C0, C1, C2 = 47.1346499, -33.7665655, 6.2541999
DT = 0.005
MASS = 0.0190534
HEAT = 0.02
RATE = 0.12

F32 = jnp.float32
OWN = 24
PAD = 16
ROWS = 48
FLAT = PAD + ROWS + PAD
FIRST, BLOCKS = 6, 5

OFFSETS = sorted(
    (
        (nx, ny, nz)
        for nx in range(-3, 4)
        for ny in range(-3, 4)
        for nz in range(-3, 4)
        if nx % 2 == ny % 2 == nz % 2 and 0 < nx * nx + ny * ny + nz * nz <= 12
    ),
    key=lambda n: (n[0] ** 2 + n[1] ** 2 + n[2] ** 2 > 8, n[1], n[2], n[0]),
)
NEAR = 26
NEAR_LIMIT = 0.42**2
FAR_LIMIT = 0.96**2


def combos(total):
    found = []
    for _, ny, nz in OFFSETS[:total]:
        if (ny, nz) != (0, 0) and (ny, nz) not in found:
            found.append((ny, nz))
    return found


SHIFTS = combos(len(OFFSETS))
SLOT = {c: i for i, c in enumerate(SHIFTS)}
SLOT[0, 0] = len(SHIFTS)
SIDES = [(a, b) for a in (-1, 0, 1) for b in (-1, 0, 1) if (a, b) != (0, 0)]
SOURCE, CODE, PLANE, BACK, HELD = 0, 20, 41, 44, 45
TABLES = 48


def ring(d, n):
    return min(d % n, -d % n)


def hops(a, b):
    most = 0
    for mx in range(NGX):
        for my in range(NGY):
            px, py = (mx + a) % NGX, (my + b) % NGY
            rows = ring(px - mx, 4) + ring(py // 4 - my // 4, 4)
            depth = (py // 2 % 2 - my // 2 % 2) * 2 + px // 4 - mx // 4
            most = max(most, rows + ring(depth, 4))
    return most


def is_near(a, b):
    return ring(a, NGX) + ring(b, NGY) <= SUB


PEERS = sorted(
    ((a, b) for a in range(NGX) for b in range(NGY) if (a, b) != (0, 0)),
    key=lambda p: -hops(*p) + (0 if is_near(*p) else 1.5),
)
NEAR_ROWS = 1 + sum(is_near(*p) for p in PEERS)
FAR_ROWS = NGX * NGY - NEAR_ROWS


def column_weights():
    keep, powers = np.zeros((NGX, NGY)), []
    keep[0, 0] = 1.0
    for _ in range(SUB + 1):
        powers.append(keep)
        beside = sum(np.roll(keep, d, axis) for axis in (0, 1) for d in (1, -1))
        keep = (1 - 6 * RATE) * keep + RATE * beside
    return [
        sum(math.comb(SUB, c) * math.comb(c, (c - d) // 2) * RATE**c * powers[SUB - c] for c in range(d, SUB + 1, 2))
        for d in range(SUB + 1)
    ]


WEIGHTS = column_weights()
TERMS = [
    (c, a, h) for c in range(SUB + 1) for a in range(NGX) for h in range(2)
    if np.any(WEIGHTS[c][a, 8 * h : 8 * h + 8] != 0)
]


def spread(x, index):
    return jnp.take_along_axis(x, index, axis=1, mode="promise_in_bounds")


def body(
    u_in, v_in, noise, heat_in, pairs_in, count,
    u_out, v_out, heat_out, flag_out, heat_same, pairs_same,
    own, packed, arrive_x, arrive_y, top, grid, grid_turned, near, far, weigh, column, row, win, shifted, mask, live_win, vel, kick, field,
    raw, back, heat, pairs, live_count, lanes,
    in_sem, halo_send, halo_recv, all_send, all_recv, far_recv, junk,
):
    mx, my = lax.axis_index("gx"), lax.axis_index("gy")
    gxs = [lax.rem(mx + d, NGX) for d in range(NGX)]
    gys = [lax.rem(my + d, NGY) for d in range(NGY)]
    gxs_back = [lax.rem(NGX + d - mx, NGX) for d in range(NGX)]
    peers = [(gxs[a], gys[b]) for a, b in PEERS]
    sides = [(gxs[a % NGX], gys[b % NGY]) for a, b in SIDES]

    barrier = pltpu.get_barrier_semaphore()
    for peer in peers:
        pl.semaphore_signal(barrier, inc=1, device_id=peer, device_id_type=MESH)

    loads = [
        pltpu.make_async_copy(pairs_in, pairs, in_sem.at[0]),
        pltpu.make_async_copy(heat_in, heat, in_sem.at[1]),
        pltpu.make_async_copy(count, live_count, in_sem.at[2]),
    ]
    for ix in range(2):
        for iy in range(2):
            spot = pl.ds(3 * ix, 3)
            at = 3 + 3 * (2 * ix + iy)
            loads += [
                pltpu.make_async_copy(u_in.at[:, ix, :, iy], raw.at[iy, pl.ds(0, 3), spot], in_sem.at[at]),
                pltpu.make_async_copy(v_in.at[:, ix, :, iy], raw.at[iy, pl.ds(3, 3), spot], in_sem.at[at + 1]),
            ] + [
                pltpu.make_async_copy(
                    noise.at[n, :, ix, :, iy], raw.at[iy, pl.ds(6 + 3 * n, 3), spot], in_sem.at[15 + 4 * n + 2 * ix + iy]
                )
                for n in range(STEPS)
            ]
    for copy in loads:
        copy.start()

    rows8 = lax.broadcasted_iota(jnp.int32, (8, TILE), 0)
    lane8 = lax.broadcasted_iota(jnp.int32, (8, TILE), 1)
    hz = lane8 % 8
    odd = hz % 2 == 1
    inside = (lane8 >= 32) & (lane8 < 96)
    zero8 = jnp.zeros((8, TILE), F32)

    for k in range(4):
        win[k] = jnp.zeros((FLAT, TILE), F32)
    live_win[...] = jnp.zeros((FLAT, TILE), F32)
    for i in range(len(SHIFTS)):
        for k in range(4):
            shifted[i, k, 0:PAD] = jnp.zeros((PAD, TILE), F32)
            shifted[i, k, PAD + ROWS : FLAT] = jnp.zeros((PAD, TILE), F32)

    cell = lane8 // 8
    for i, (ny, nz) in enumerate(SHIFTS + [(0, 0)]):
        dy = (ny - ny % 2) // 2 + (hz % 2 if ny % 2 else 0)
        if i < len(SHIFTS):
            lanes[SOURCE + i] = (cell + dy + 16) % 16 * 8 + (hz + nz + 8) % 8
        above = (cell % 4 + dy + 4) // 4 - 1
        lanes[CODE + i] = lane8 // 32 * 32 + 9 + 3 * (above + 1) + (hz + nz + 8) // 8
    layer = (3 * lane8 + 15) // 16
    lanes[BACK] = layer % 8
    for i in range(OWN // 8):
        t = (rows8 + 8 * i) % 3
        lanes[PLANE + i] = (t * 8 + hz) * 16 // 3
        lanes[HELD + i] = jnp.where((layer * 16 // 3 == lane8) & (layer // 8 == t), 1, 0)
    for i, (c, a, h) in enumerate(TERMS):
        value = zero8
        for j in range(8):
            if WEIGHTS[c][a, 8 * h + j]:
                value = jnp.where(rows8 == j, float(WEIGHTS[c][a, 8 * h + j]), value)
        weigh[i] = value

    for copy in loads:
        copy.wait()

    def gathered(c, cell):
        low, high = raw[0, c], raw[1, c]
        low = low if cell == 1 else pltpu.roll(low, (32 * (1 - cell)) % TILE, 1)
        high = high if cell == 2 else pltpu.roll(high, (32 * (2 - cell)) % TILE, 1)
        return jnp.where(lane8 < 64, low, high)

    def unpack(c, target):
        for cell in range(4):
            value = jnp.where(inside, gathered(c, cell), 0.0)
            for ix in range(2):
                start = (4 * ix + cell) * 3
                target[start : start + 3] = value[3 * ix : 3 * ix + 3]

    for k in range(3):
        unpack(k, own.at[0, k])
        unpack(3 + k, vel.at[k])

    def pack(n, values, start, size):
        group = lax.broadcasted_iota(jnp.int32, (size, TILE), 1) // 32
        for half in range(2):
            out = None
            for k, value in enumerate(values):
                turn = (32 * (k - 1 - half)) % TILE
                value = pltpu.roll(value, turn, 1) if turn else value
                out = value if out is None else jnp.where(group == k, value, out)
            packed[n, half, start : start + size] = out

    p_row = lax.broadcasted_iota(jnp.int32, (OWN, PAIRS), 0)
    p_lane = lax.broadcasted_iota(jnp.int32, (TILE, PAIRS), 0)
    slot = lax.broadcasted_iota(jnp.int32, (OWN, PAIRS), 1)
    tile, code = pairs[0:1, :], pairs[1:2, :]
    named = (tile // 6 * 3 + tile % 3 == p_row // 12 * 3 + p_row % 3) & (slot < live_count[0, 0])
    coded = tile // 3 % 2 * 32 + 32 + code == p_lane
    own[0, 3] = lax.dot_general(
        jnp.where(named, 1.0, 0.0).astype(jnp.bfloat16),
        jnp.where(coded, 1.0, 0.0).astype(jnp.bfloat16),
        (((1,), (1,)), ((), ())),
        preferred_element_type=F32,
    )
    pack(0, [own[0, k] for k in range(4)], 0, OWN)
    top[...] = zero8
    for i in range(NGX):
        row[0, 0:1, NGY * i : NGY * (i + 1)] = heat[i : i + 1, :]

    pl.semaphore_wait(barrier, len(peers))

    def halo_copies(n, channels):
        copies = []
        for i, (a, b) in enumerate(SIDES):
            part = pl.ds(12 if a > 0 else 0, 12) if a else pl.ds(0, OWN)
            if b:
                src = packed.at[n, (b + 1) // 2, part]
                dst = arrive_y.at[n, i, pl.ds(0, 12 if a else OWN)]
            else:
                src = own.at[n, pl.ds(0, channels), part]
                dst = arrive_x.at[n, (a + 1) // 2, pl.ds(0, channels)]
            copies.append(
                pltpu.make_async_remote_copy(
                    src_ref=src, dst_ref=dst, send_sem=halo_send.at[n, i], recv_sem=halo_recv.at[n, i],
                    device_id=sides[i], device_id_type=MESH,
                )
            )
        return copies

    def send_all(g, first):
        src = row.at[g, pl.ds(0, 1)]
        for (a, b), peer in zip(PEERS, peers):
            if first:
                dst, done = grid.at[mx, pl.ds(my, 1)], all_recv.at[0]
            else:
                there = (-a % NGX, pl.ds(-b % NGY, 1))
                dst = (near if is_near(a, b) else far).at[(g, *there)]
                done = (all_recv if is_near(a, b) else far_recv).at[g]
            pltpu.make_async_remote_copy(
                src_ref=src, dst_ref=dst, send_sem=all_send.at[g], recv_sem=done,
                device_id=peer, device_id_type=MESH,
            ).start()
        mine = grid.at[mx, pl.ds(my, 1)] if first else near.at[g, 0, pl.ds(0, 1)]
        pltpu.make_async_copy(src, mine, all_recv.at[g]).start()
        pltpu.make_async_copy(src, junk.at[pl.ds(g, 1)], all_send.at[g]).start()

    def wait_rows(sem, count):
        part = junk.at[pl.ds(0, count)]
        pltpu.make_async_copy(part, part, sem).wait()

    def place(n, channel, target):
        for start, size, a in ((0, 12, 1), (12, 24, 0), (36, 12, -1)):
            low = arrive_y[n, SIDES.index((a, 1)), 0:size]
            high = arrive_y[n, SIDES.index((a, -1)), 0:size]
            low = pltpu.roll(low, TILE - 32 * channel, 1) if channel else low
            high = pltpu.roll(high, 96 - 32 * channel, 1) if channel < 3 else high
            middle = arrive_x[n, (a + 1) // 2, channel] if a else own[n, channel]
            lane = lax.broadcasted_iota(jnp.int32, (size, TILE), 1)
            target[PAD + start : PAD + start + size] = jnp.where(
                lane < 32, low, jnp.where(lane < 96, middle, high)
            )

    carry = {n: (hz < n if n > 0 else hz >= 8 + n) for n in (-3, -2, -1, 1, 2, 3)}

    def stage(total, k):
        wanted = combos(total)
        for block in range(ROWS // 8):
            r = PAD + 8 * block
            t = (rows8 + 8 * block) % 3
            middle = win[k, r : r + 8]
            up = jnp.where(t < 2, win[k, r + 1 : r + 9], win[k, r - 2 : r + 6])
            down = jnp.where(t > 0, win[k, r - 1 : r + 7], win[k, r + 2 : r + 10])
            for depth in sorted({nz for _, nz in wanted}):
                source = jnp.where(carry[depth], up if depth > 0 else down, middle) if depth else middle
                for ny, nz in wanted:
                    if nz == depth:
                        i = SLOT[ny, nz]
                        shifted[i, k, r : r + 8] = spread(source, lanes[SOURCE + i])

    def neighbour(o, k, r):
        nx, ny, nz = OFFSETS[o]
        i = SLOT[ny, nz]
        get = (lambda q: shifted[i, k, q : q + 8]) if (ny, nz) != (0, 0) else (lambda q: win[k, q : q + 8])
        if nx % 2 == 0:
            return get(r + 3 * (nx // 2))
        return jnp.where(odd, get(r + 3 * ((nx + 1) // 2)), get(r + 3 * ((nx - 1) // 2)))

    def pair(o, r, mine):
        delta = [
            (mine[k] - (0.5 * EDGE) * n) - neighbour(o, k, r) for k, n in enumerate(OFFSETS[o])
        ]
        square = delta[0] * delta[0] + delta[1] * delta[1] + delta[2] * delta[2]
        inverse = lax.rsqrt(square)
        return delta, square * inverse, inverse

    def masks(first, last):
        for block in range(BLOCKS):
            start = FIRST + 8 * block
            cell = (rows8 + start) // 3 % 4
            known = live_win[PAD + start : PAD + start + 8]
            over = {}
            for nx in range(-3, 4):
                dx = cell + (nx // 2 if nx % 2 == 0 else (nx - 1) // 2 + hz % 2)
                over[nx] = jnp.where(dx > 3, 9, jnp.where(dx < 0, -9, 0))
            for o in range(first, last):
                nx, ny, nz = OFFSETS[o]
                mask[o, 8 * block : 8 * block + 8] = spread(known, lanes[CODE + SLOT[ny, nz]] + over[nx])

    def step(n, total):
        for k in range(3):
            place(n, k, win.at[k])
        for k in range(3):
            stage(total, k)
        for block in range(BLOCKS):
            r = PAD + FIRST + 8 * block
            mine = [win[k, r : r + 8] for k in range(3)]
            density = zero8
            for o in range(total):
                _, distance, _ = pair(o, r, mine)
                gap = jnp.minimum(distance - RC, 0.0)
                density = density + mask[o, 8 * block : 8 * block + 8] * (gap * gap)
            win[3, r : r + 8] = -EMBED * lax.rsqrt(density)
        stage(total, 3)
        forces = []
        for block in range(OWN // 8):
            r = PAD + 12 + 8 * block
            q = 12 - FIRST + 8 * block
            mine = [win[k, r : r + 8] for k in range(3)]
            slope = win[3, r : r + 8]
            total_force = [zero8] * 3
            for o in range(total):
                delta, distance, inverse = pair(o, r, mine)
                gap = jnp.minimum(distance - RC, 0.0)
                close = jnp.minimum(distance - RP, 0.0)
                quad = (2 * C0 - RP * C1) + distance * ((3 * C1 - 2 * RP * C2) + (4 * C2) * distance)
                scalar = close * quad + (slope + neighbour(o, 3, r)) * gap
                scalar = scalar * inverse * mask[o, q : q + 8]
                total_force = [f - scalar * d for f, d in zip(total_force, delta)]
            forces.append([jnp.where(inside, f, 0.0) for f in total_force])
        return forces

    def diffuse(t):
        for _ in range(SUB):
            beside = jnp.concatenate([t[1:], t[:1]], axis=0) + jnp.concatenate([t[-1:], t[:-1]], axis=0)
            beside = beside + pltpu.roll(t, 1, 1) + pltpu.roll(t, NGY - 1, 1)
            beside = beside + pltpu.roll(t, 1, 2) + pltpu.roll(t, TILE - 1, 2)
            t = t + RATE * (beside - 6.0 * t)
        return t

    def near_part(g, a, h, other):
        most = SUB - ring(a, NGX)
        within = rows8 <= most if h == 0 else rows8 >= 8 - most
        return jnp.where(within, near[g, a, 8 * h : 8 * h + 8], other)

    def weighed(get, marked):
        sums = [zero8] * (SUB + 1)
        for i, (c, a, h) in enumerate(TERMS):
            sums[c] = sums[c] + weigh[i] * get(a, h)
        if marked:
            sums = [jnp.where(lane8 == 1, 0.0, v) for v in sums]
        total = sums[0]
        for d in range(1, SUB + 1):
            total = total + (pltpu.roll(sums[d], d, 1) + pltpu.roll(sums[d], TILE - d, 1))
        return total

    def field_rows(a, h):
        return field[a, 8 * h : 8 * h + 8]

    def gathered_rows(g):
        return jnp.stack([
            jnp.concatenate([near_part(g, a, h, far[g, a, 8 * h : 8 * h + 8]) for h in range(2)], axis=0)
            for a in range(NGX)
        ])

    def deposit(g):
        lane3 = lax.broadcasted_iota(jnp.int32, (NGX, NGY, TILE), 2)
        added = jnp.where(lane3 == 1, 0.0, gathered_rows(g)) * (1.0 / HEAT)
        return diffuse(field[...] + added)

    def advance(n, forces):
        local = jnp.broadcast_to(jnp.sum(column[...], axis=0, keepdims=True), (8, TILE))
        power = []
        for block in range(OWN // 8):
            at = slice(8 * block, 8 * block + 8)
            push = jnp.sqrt((2.0 * MASS / DT) * spread(local, lanes[PLANE + block]))
            energy, places = zero8, []
            for k in range(3):
                speed = vel[k, at]
                speed = speed + (DT / MASS) * (forces[block][k] - MASS * speed + push * kick[n, k, at])
                vel[k, at] = speed
                moved = win[k, PAD + 12 + 8 * block : PAD + 20 + 8 * block] + DT * speed
                own[n + 1, k, at] = moved
                places.append(moved)
                energy = energy + speed * speed
            pack(n + 1, places, 8 * block, 8)
            power.append(energy)
        return power

    def energies(n, power):
        out = zero8
        index = [lanes[BACK] + (32 + 8 * i) for i in range(8)]
        for block in range(OWN // 8):
            parts = [spread(power[block], i) for i in index]
            while len(parts) > 1:
                parts = [a + b for a, b in zip(parts[::2], parts[1::2])]
            out = out + jnp.where(lanes[HELD + block] > 0, parts[0], 0.0)
        out = (MASS * DT) * jnp.sum(out, axis=0, keepdims=True)
        row[n + 1, 0:1] = jnp.where(lane8[0:1] == 1, top[0:1], out)

    def reach(n):
        most = zero8
        for block in range(OWN // 8):
            at = slice(8 * block, 8 * block + 8)
            square = sum(own[n + 1, k, at] * own[n + 1, k, at] for k in range(3))
            most = jnp.maximum(most, jnp.where(inside, square, 0.0))
        most = jnp.max(jnp.max(most, axis=1, keepdims=True), axis=0, keepdims=True)
        top[...] = jnp.broadcast_to(most, (8, TILE))

    def full_step(n, total):
        forces = step(n, total)

        @pl.when(n == 0)
        def _():
            wait_rows(all_recv.at[0], NGX * NGY)
            turn = jnp.transpose(grid[...].reshape(TILE, TILE)).reshape(NGX, NGY, TILE)
            grid_turned[...] = turn
            column[0:1] = grid_turned[mx, pl.ds(my, 1), :]
            column[1:8] = jnp.zeros((7, TILE), F32)

        @pl.when(n > 0)
        def _():
            wait_rows(all_recv.at[n], NEAR_ROWS)
            arrived = weighed(lambda a, h: near_part(n, a, h, 0.0), True)
            column[...] = column[...] + (1.0 / HEAT) * arrived

        power = advance(n, forces)

        @pl.when(n < STEPS - 1)
        def _():
            for c in halo_copies(n + 1, 3):
                c.start()

        energies(n, power)
        send_all(n + 1, False)

        reach(n)
        @pl.when(n == 0)
        def _():
            masks(NEAR, len(OFFSETS))
            for a in range(NGX):
                field[a] = pltpu.roll(grid_turned[gxs[a]], lax.rem(NGY - my, NGY), 0)

        @pl.when(n > 0)
        def _():
            wait_rows(far_recv.at[n], FAR_ROWS)
            field[...] = deposit(n)

        column[...] = weighed(field_rows, False)
        wait_rows(all_send.at[n], NGX * NGY)

        @pl.when(n < STEPS - 1)
        def _():
            waits = halo_copies(n + 1, 3)
            for c in waits:
                c.wait_recv()
            for c in waits:
                c.wait_send()

    first = halo_copies(0, 4)
    for c in first:
        c.start()
    send_all(0, True)
    for n in range(STEPS):
        for k in range(3):
            unpack(6 + 3 * n + k, kick.at[n, k])
    for c in first:
        c.wait_recv()
    for c in first:
        c.wait_send()

    place(0, 3, live_win)
    masks(0, NEAR)

    lax.fori_loop(0, 2, lambda n, c: (full_step(n, NEAR), c)[1], 0)
    lax.fori_loop(2, 4, lambda n, c: (full_step(n, len(OFFSETS)), c)[1], 0)

    for c in range(6):
        held = own.at[STEPS, c] if c < 3 else vel.at[c - 3]
        for cell in range(4):
            for ix in range(2):
                start = (4 * ix + cell) * 3
                raw[0, cell, 3 * ix : 3 * ix + 3] = held[start : start + 3]
        for iy in range(2):
            value = zero8
            for cell in range(4):
                part = raw[0, cell]
                part = part if cell == 1 + iy else pltpu.roll(part, (32 * (cell - 1 - iy)) % TILE, 1)
                value = jnp.where(lane8 // 32 == cell, part, value)
            back[iy, c] = value
    stores = [
        pltpu.make_async_copy(heat, heat_same, in_sem.at[1]),
        pltpu.make_async_copy(pairs, pairs_same, in_sem.at[0]),
    ]
    for ix in range(2):
        for iy in range(2):
            spot = pl.ds(3 * ix, 3)
            at = 3 + 3 * (2 * ix + iy)
            stores += [
                pltpu.make_async_copy(back.at[iy, pl.ds(0, 3), spot], u_out.at[:, ix, :, iy], in_sem.at[at]),
                pltpu.make_async_copy(back.at[iy, pl.ds(3, 3), spot], v_out.at[:, ix, :, iy], in_sem.at[at + 1]),
            ]
    for copy in stores:
        copy.start()
    lane1 = lane8[0:1] == 1
    wait_rows(all_recv.at[STEPS], NEAR_ROWS)
    wait_rows(far_recv.at[STEPS], FAR_ROWS)
    wait_rows(all_send.at[STEPS], NGX * NGY)
    most = [jnp.max(gathered_rows(g), axis=0) for g in range(2, STEPS + 1)]
    most = [jnp.max(v, axis=0, keepdims=True) for v in most]
    fine = (most[0] <= NEAR_LIMIT) & (jnp.maximum(most[1], most[2]) <= FAR_LIMIT)
    flag_out[0, 0] = jnp.sum(jnp.where(lane1 & fine, 1.0, 0.0))
    field[...] = deposit(STEPS)
    mine = lax.broadcasted_iota(jnp.int32, (NGY, TILE), 1) == mx * NGY + my
    planes = [jnp.where(mine, pltpu.roll(field[gxs_back[i]], my, 0), 0.0) for i in range(NGX)]
    heat_out[0] = jnp.sum(jnp.stack(planes), axis=2)
    for copy in stores:
        copy.wait()


def fast(displacement, velocity, noise, electron_temp, pair_list, pair_count):
    turn = lambda v: jnp.swapaxes(v, -3, -2)
    brick = (3, 2, TZ, 2, TILE)
    hbm = pl.BlockSpec(memory_space=pltpu.HBM)
    vmem = pl.BlockSpec(memory_space=pltpu.VMEM)
    total = len(OFFSETS)
    u, v, heat, flag, heat_same, pairs_same = pl.pallas_call(
        body,
        out_shape=(
            jax.ShapeDtypeStruct(brick, F32),
            jax.ShapeDtypeStruct(brick, F32),
            jax.ShapeDtypeStruct((1, NGX, NGY), F32),
            jax.ShapeDtypeStruct((1, 1), F32),
            jax.ShapeDtypeStruct((NGX, NGY), F32),
            jax.ShapeDtypeStruct((2, PAIRS), jnp.int32),
        ),
        in_specs=[hbm] * 6,
        out_specs=(hbm, hbm, vmem, pl.BlockSpec(memory_space=pltpu.SMEM), hbm, hbm),
        scratch_shapes=[
            pltpu.VMEM((STEPS + 1, 4, OWN, TILE), F32),
            pltpu.VMEM((STEPS + 1, 2, OWN, TILE), F32),
            pltpu.VMEM((STEPS, 2, 4, 12, TILE), F32),
            pltpu.VMEM((STEPS, 8, OWN, TILE), F32),
            pltpu.VMEM((8, TILE), F32),
            pltpu.VMEM((NGX, NGY, TILE), F32),
            pltpu.VMEM((NGX, NGY, TILE), F32),
            pltpu.VMEM((STEPS + 1, NGX, NGY, TILE), F32),
            pltpu.VMEM((STEPS + 1, NGX, NGY, TILE), F32),
            pltpu.VMEM((len(TERMS), 8, TILE), F32),
            pltpu.VMEM((8, TILE), F32),
            pltpu.VMEM((STEPS + 1, 8, TILE), F32),
            pltpu.VMEM((4, FLAT, TILE), F32),
            pltpu.VMEM((len(SHIFTS), 4, FLAT, TILE), F32),
            pltpu.VMEM((total, 8 * BLOCKS, TILE), F32),
            pltpu.VMEM((FLAT, TILE), F32),
            pltpu.VMEM((3, OWN, TILE), F32),
            pltpu.VMEM((STEPS, 3, OWN, TILE), F32),
            pltpu.VMEM((NGX, NGY, TILE), F32),
            pltpu.VMEM((2, 18, 8, TILE), F32),
            pltpu.VMEM((2, 6, 8, TILE), F32),
            pltpu.VMEM((NGX, NGY), F32),
            pltpu.VMEM((2, PAIRS), jnp.int32),
            pltpu.SMEM((1, 1), jnp.int32),
            pltpu.VMEM((TABLES, 8, TILE), jnp.int32),
            pltpu.SemaphoreType.DMA((15 + 4 * STEPS,)),
            pltpu.SemaphoreType.DMA((STEPS, 8)),
            pltpu.SemaphoreType.DMA((STEPS, 8)),
            pltpu.SemaphoreType.DMA((STEPS + 1,)),
            pltpu.SemaphoreType.DMA((STEPS + 1,)),
            pltpu.SemaphoreType.DMA((STEPS + 1,)),
            pltpu.VMEM((NGX * NGY, TILE), F32),
        ],
        compiler_params=pltpu.CompilerParams(
            collective_id=0, has_side_effects=True, vmem_limit_bytes=60 << 20
        ),
    )(turn(displacement), turn(velocity), turn(noise), electron_temp[0], pair_list[0, 0], pair_count)
    return (turn(u), turn(v), heat), flag, (heat_same[None], pairs_same[None, None])


def padded_2(values, sides, width):
    for axis, dim in sides:
        count = lax.axis_size(axis)
        forward = [(i, (i + 1) % count) for i in range(count)]
        backward = [(target, source) for source, target in forward]
        low = lax.ppermute(lax.slice_in_dim(values, values.shape[dim] - width, None, axis=dim), axis, forward)
        high = lax.ppermute(lax.slice_in_dim(values, 0, width, axis=dim), axis, backward)
        values = jnp.concatenate([low, values, high], axis=dim)
    return values


def lattice_sites():
    serial = jnp.arange(TILE, dtype=jnp.int32)
    cell = serial // 2
    corners = jnp.stack([cell // 16, cell // 4 % 4, cell % 4])
    return EDGE * (corners.astype(F32) + ((serial % 2).astype(F32) * 0.5)[None, :])


def pair_geometry(flat, tile_index, code, lattice):
    t, iy, ix = tile_index % TZ, tile_index // TZ % 2, tile_index // (TZ * 2)
    ex, ey, ez = code // 9, code // 3 % 3, code % 3
    own_index = ((ix + 1) * 4 + iy + 1) * TZ + t
    other_index = ((ix + ex) * 4 + iy + ey) * TZ + (t + ez - 1 + TZ) % TZ
    own_tile = lax.dynamic_index_in_dim(flat, own_index, 1, keepdims=False)
    other_tile = lax.dynamic_index_in_dim(flat, other_index, 1, keepdims=False)
    offset = jnp.stack([ex - 1, ey - 1, ez - 1]).astype(F32) * (4 * EDGE)
    delta = (lattice + own_tile)[:, :, None] - (lattice + other_tile + offset[:, None])[:, None, :]
    square = jnp.sum(delta * delta, axis=0)
    serial = jnp.arange(TILE, dtype=jnp.int32)
    same = (code == 13) & (serial[:, None] == serial[None, :])
    return delta, jnp.sqrt(jnp.where(same, 100.0, square)), own_index, other_index


def density_term(flat, lattice, tile_index, code):
    _, distance, _, _ = pair_geometry(flat, tile_index, code, lattice)
    gap = distance - RC
    return jnp.sum(jnp.where(distance < RC, gap * gap, 0.0), axis=1)[None]


def force_term(flat, embed, lattice, tile_index, code):
    delta, distance, own_index, other_index = pair_geometry(flat, tile_index, code, lattice)
    own_embed = lax.dynamic_index_in_dim(embed, own_index, 0, keepdims=False)
    other_embed = lax.dynamic_index_in_dim(embed, other_index, 0, keepdims=False)
    gap = distance - RP
    poly = C0 + C1 * distance + C2 * distance * distance
    slope = jnp.where(distance < RP, 2.0 * gap * poly + gap * gap * (C1 + 2.0 * C2 * distance), 0.0)
    dens = jnp.where(distance < RC, 2.0 * (distance - RC), 0.0)
    scalar = (slope + (own_embed[:, None] + other_embed[None, :]) * dens) / distance
    return -jnp.sum(scalar[None] * delta, axis=2)


def sweep(term, channels, table, total):
    def visit(i, running):
        entry = lax.dynamic_slice_in_dim(table, i, 1, 1)
        u = entry[0, 0]
        value = jnp.where(i < total, term(u, entry[1, 0]), 0.0)
        old = lax.dynamic_slice_in_dim(running, u, 1, 1)
        return lax.dynamic_update_slice_in_dim(running, old + value[:, None], u, 1)

    running = lax.fori_loop(0, PAIRS, visit, jnp.zeros((channels, TILES, TILE), F32))
    return running.reshape(channels, 2, 2, TZ, TILE)


def slow(displacement, velocity, noise, electron_temp, pair_list, pair_count):
    lattice = lattice_sites()
    table, total = pair_list[0, 0], pair_count[0, 0]
    owners = NGX * NGY
    serial = np.arange(TZ * TILE)
    layer = serial // TILE * 8 + serial % 8
    onehot = jnp.asarray((layer * owners // 24)[:, None] == np.arange(owners)[None, :])
    axes = (("gx", 1), ("gy", 2))

    def one(n, carry):
        positions, speeds, heat = carry
        arrived = lax.all_to_all(heat.reshape(1, owners), ("gx", "gy"), split_axis=1, concat_axis=0, tiled=True)
        local = jnp.sum(jnp.where(onehot, arrived.reshape(1, owners), 0.0), axis=1).reshape(1, 1, 1, TZ, TILE)
        flat = padded_2(positions, axes, 1).reshape(3, 16 * TZ, TILE)
        density = sweep(partial(density_term, flat, lattice), 1, table, total)
        embed = padded_2(-EMBED / (2.0 * jnp.sqrt(density)), axes, 1).reshape(16 * TZ, TILE)
        force = sweep(partial(force_term, flat, embed, lattice), 3, table, total)
        kicker = jnp.sqrt(2.0 * MASS * local / DT) * lax.dynamic_index_in_dim(noise, n, 0, keepdims=False)
        speeds = speeds + DT / MASS * (force - MASS * speeds + kicker)
        positions = positions + DT * speeds
        power = MASS * DT * jnp.sum(speeds * speeds, axis=0)
        power = jnp.sum(power, axis=(0, 1)).reshape(-1, 1)
        energy = jnp.sum(jnp.where(onehot, power, 0.0), axis=0)
        arrived = lax.all_to_all(energy.reshape(owners, 1), ("gx", "gy"), split_axis=0, concat_axis=1, tiled=True)
        heat = heat + arrived.reshape(1, NGX, NGY) / HEAT

        def relax(_, heat):
            padded = padded_2(heat, ((("gx", "gy"), 0),), 1)
            beside = padded[2:] + padded[:-2] + jnp.roll(heat, 1, 1) + jnp.roll(heat, -1, 1)
            beside = beside + jnp.roll(heat, 1, 2) + jnp.roll(heat, -1, 2)
            return heat + RATE * (beside - 6.0 * heat)

        return positions, speeds, lax.fori_loop(0, SUB, relax, heat)

    return lax.fori_loop(0, STEPS, one, (displacement, velocity, electron_temp))


def per_device(*arguments):
    results, flag, (heat, pairs) = fast(*arguments)
    displacement, velocity, noise, _, _, count = arguments
    return lax.cond(
        flag[0, 0] > 0.5, lambda: results, lambda: slow(displacement, velocity, noise, heat, pairs, count)
    )


def solution(mesh):
    brick = P(None, "gx", "gy", None, None)
    placed = (
        brick,
        brick,
        P(None, None, "gx", "gy", None, None),
        P(("gx", "gy"), None, None),
        P("gx", "gy", None, None),
        P("gx", "gy"),
    )
    return jax.shard_map(
        per_device, mesh=mesh, in_specs=placed, out_specs=(brick, brick, P(("gx", "gy"), None, None)), check_vma=False
    )
```

```python
import math
from functools import partial

import jax
import jax.numpy as jnp
import numpy as np
from jax import lax
from jax.experimental import pallas as pl
from jax.experimental.pallas import tpu as pltpu
from jax.sharding import PartitionSpec as P

MESH = pl.DeviceIdType.MESH
NGX, NGY = 8, 16
TZ, TILE, TILES, STEPS, SUB = 3, 128, 12, 4, 6
PAIRS = 324

EDGE = 3.1652
RC = 4.400224
EMBED = 1.896373
RP = 3.25
C0, C1, C2 = 47.1346499, -33.7665655, 6.2541999
DT = 0.005
MASS = 0.0190534
HEAT = 0.02
RATE = 0.12

F32 = jnp.float32
OWN = 24
PAD = 16
ROWS = 48
FLAT = PAD + ROWS + PAD
FIRST, BLOCKS = 4, 5

OFFSETS = sorted(
    (
        (nx, ny, nz)
        for nx in range(-3, 4)
        for ny in range(-3, 4)
        for nz in range(-3, 4)
        if nx % 2 == ny % 2 == nz % 2 and 0 < nx * nx + ny * ny + nz * nz <= 12
    ),
    key=lambda n: (n[0] ** 2 + n[1] ** 2 + n[2] ** 2 > 8, n[1], n[2], n[0]),
)
NEAR = 26
NEAR_LIMIT = 0.42**2
FAR_LIMIT = 0.96**2


def combos(total):
    found = []
    for _, ny, nz in OFFSETS[:total]:
        if (ny, nz) != (0, 0) and (ny, nz) not in found:
            found.append((ny, nz))
    return found


SHIFTS = combos(len(OFFSETS))
SLOT = {c: i for i, c in enumerate(SHIFTS)}
SLOT[0, 0] = len(SHIFTS)
SIDES = [(a, b) for a in (-1, 0, 1) for b in (-1, 0, 1) if (a, b) != (0, 0)]
SOURCE, CODE, PLANE, BACK, HELD = 0, 20, 41, 44, 45
TABLES = 48


def ring(d, n):
    return min(d % n, -d % n)


def hops(a, b):
    most = 0
    for mx in range(NGX):
        for my in range(NGY):
            px, py = (mx + a) % NGX, (my + b) % NGY
            rows = ring(px - mx, 4) + ring(py // 4 - my // 4, 4)
            depth = (py // 2 % 2 - my // 2 % 2) * 2 + px // 4 - mx // 4
            most = max(most, rows + ring(depth, 4))
    return most


def is_near(a, b):
    return ring(a, NGX) + ring(b, NGY) <= SUB


PEERS = sorted(
    ((a, b) for a in range(NGX) for b in range(NGY) if (a, b) != (0, 0)),
    key=lambda p: -hops(*p) + (0 if is_near(*p) else 1.5),
)
NEAR_ROWS = 1 + sum(is_near(*p) for p in PEERS)
FAR_ROWS = NGX * NGY - NEAR_ROWS


def column_weights():
    keep, powers = np.zeros((NGX, NGY)), []
    keep[0, 0] = 1.0
    for _ in range(SUB + 1):
        powers.append(keep)
        beside = sum(np.roll(keep, d, axis) for axis in (0, 1) for d in (1, -1))
        keep = (1 - 6 * RATE) * keep + RATE * beside
    return [
        sum(math.comb(SUB, c) * math.comb(c, (c - d) // 2) * RATE**c * powers[SUB - c] for c in range(d, SUB + 1, 2))
        for d in range(SUB + 1)
    ]


WEIGHTS = column_weights()
TERMS = [
    (c, a, h) for c in range(SUB + 1) for a in range(NGX) for h in range(2)
    if np.any(WEIGHTS[c][a, 8 * h : 8 * h + 8] != 0)
]


def spread(x, index):
    return jnp.take_along_axis(x, index, axis=1, mode="promise_in_bounds")


def body(
    u_in, v_in, noise, heat_in, pairs_in, count,
    u_out, v_out, heat_out, flag_out, heat_same, pairs_same, u_same, v_same,
    own, packed, arrive_x, arrive_y, top, grid, grid_turned, near, far, weigh, column, row, win, shifted, mask, terms, live_win, vel, kick, field,
    raw, back, heat, pairs, live_count, lanes,
    in_sem, halo_send, halo_recv, all_send, all_recv, far_recv, junk,
):
    mx, my = lax.axis_index("gx"), lax.axis_index("gy")
    gxs = [lax.rem(mx + d, NGX) for d in range(NGX)]
    gys = [lax.rem(my + d, NGY) for d in range(NGY)]
    gxs_back = [lax.rem(NGX + d - mx, NGX) for d in range(NGX)]
    peers = [(gxs[a], gys[b]) for a, b in PEERS]
    sides = [(gxs[a % NGX], gys[b % NGY]) for a, b in SIDES]

    barrier = pltpu.get_barrier_semaphore()
    for peer in peers:
        pl.semaphore_signal(barrier, inc=1, device_id=peer, device_id_type=MESH)

    loads = [
        pltpu.make_async_copy(pairs_in, pairs, in_sem.at[0]),
        pltpu.make_async_copy(heat_in, heat, in_sem.at[1]),
        pltpu.make_async_copy(count, live_count, in_sem.at[2]),
    ]
    for ix in range(2):
        for iy in range(2):
            spot = pl.ds(3 * ix, 3)
            at = 3 + 3 * (2 * ix + iy)
            loads += [
                pltpu.make_async_copy(u_in.at[:, ix, :, iy], raw.at[iy, pl.ds(0, 3), spot], in_sem.at[at]),
                pltpu.make_async_copy(v_in.at[:, ix, :, iy], raw.at[iy, pl.ds(3, 3), spot], in_sem.at[at + 1]),
            ] + [
                pltpu.make_async_copy(
                    noise.at[n, :, ix, :, iy], raw.at[iy, pl.ds(6 + 3 * n, 3), spot], in_sem.at[15 + 4 * n + 2 * ix + iy]
                )
                for n in range(STEPS)
            ]
    for copy in loads:
        copy.start()

    rows8 = lax.broadcasted_iota(jnp.int32, (8, TILE), 0)
    lane8 = lax.broadcasted_iota(jnp.int32, (8, TILE), 1)
    hz = lane8 % 8
    odd = hz % 2 == 1
    inside = (lane8 >= 32) & (lane8 < 96)
    zero8 = jnp.zeros((8, TILE), F32)

    for k in range(4):
        win[k] = jnp.zeros((FLAT, TILE), F32)
    live_win[...] = jnp.zeros((FLAT, TILE), F32)
    for i in range(len(SHIFTS)):
        for k in range(4):
            shifted[i, k, 0:PAD] = jnp.zeros((PAD, TILE), F32)
            shifted[i, k, PAD + ROWS : FLAT] = jnp.zeros((PAD, TILE), F32)

    cell = lane8 // 8
    for i, (ny, nz) in enumerate(SHIFTS + [(0, 0)]):
        dy = (ny - ny % 2) // 2 + (hz % 2 if ny % 2 else 0)
        if i < len(SHIFTS):
            lanes[SOURCE + i] = (cell + dy + 16) % 16 * 8 + (hz + nz + 8) % 8
        above = (cell % 4 + dy + 4) // 4 - 1
        lanes[CODE + i] = lane8 // 32 * 32 + 9 + 3 * (above + 1) + (hz + nz + 8) // 8
    layer = (3 * lane8 + 15) // 16
    lanes[BACK] = layer % 8
    for i in range(OWN // 8):
        t = (rows8 + 8 * i) % 3
        lanes[PLANE + i] = (t * 8 + hz) * 16 // 3
        lanes[HELD + i] = jnp.where((layer * 16 // 3 == lane8) & (layer // 8 == t), 1, 0)
    for i, (c, a, h) in enumerate(TERMS):
        value = zero8
        for j in range(8):
            if WEIGHTS[c][a, 8 * h + j]:
                value = jnp.where(rows8 == j, float(WEIGHTS[c][a, 8 * h + j]), value)
        weigh[i] = value

    for copy in loads:
        copy.wait()

    def gathered(c, cell):
        low, high = raw[0, c], raw[1, c]
        low = low if cell == 1 else pltpu.roll(low, (32 * (1 - cell)) % TILE, 1)
        high = high if cell == 2 else pltpu.roll(high, (32 * (2 - cell)) % TILE, 1)
        return jnp.where(lane8 < 64, low, high)

    def unpack(c, target):
        for cell in range(4):
            value = jnp.where(inside, gathered(c, cell), 0.0)
            for ix in range(2):
                start = (4 * ix + cell) * 3
                target[start : start + 3] = value[3 * ix : 3 * ix + 3]

    for k in range(3):
        unpack(k, own.at[0, k])
        unpack(3 + k, vel.at[k])

    def pack(n, values, start, size):
        group = lax.broadcasted_iota(jnp.int32, (size, TILE), 1) // 32
        for half in range(2):
            out = None
            for k, value in enumerate(values):
                turn = (32 * (k - 1 - half)) % TILE
                value = pltpu.roll(value, turn, 1) if turn else value
                out = value if out is None else jnp.where(group == k, value, out)
            packed[n, half, start : start + size] = out

    p_row = lax.broadcasted_iota(jnp.int32, (OWN, PAIRS), 0)
    p_lane = lax.broadcasted_iota(jnp.int32, (TILE, PAIRS), 0)
    slot = lax.broadcasted_iota(jnp.int32, (OWN, PAIRS), 1)
    tile, code = pairs[0:1, :], pairs[1:2, :]
    named = (tile // 6 * 3 + tile % 3 == p_row // 12 * 3 + p_row % 3) & (slot < live_count[0, 0])
    coded = tile // 3 % 2 * 32 + 32 + code == p_lane
    own[0, 3] = lax.dot_general(
        jnp.where(named, 1.0, 0.0).astype(jnp.bfloat16),
        jnp.where(coded, 1.0, 0.0).astype(jnp.bfloat16),
        (((1,), (1,)), ((), ())),
        preferred_element_type=F32,
    )
    pack(0, [own[0, k] for k in range(4)], 0, OWN)
    top[...] = zero8
    for i in range(NGX):
        row[0, 0:1, NGY * i : NGY * (i + 1)] = heat[i : i + 1, :]

    pl.semaphore_wait(barrier, len(peers))

    def halo_copies(n, channels):
        copies = []
        for i, (a, b) in enumerate(SIDES):
            part = pl.ds(12 if a > 0 else 0, 12) if a else pl.ds(0, OWN)
            if b:
                src = packed.at[n, (b + 1) // 2, part]
                dst = arrive_y.at[n, i, pl.ds(0, 12 if a else OWN)]
            else:
                src = own.at[n, pl.ds(0, channels), part]
                dst = arrive_x.at[n, (a + 1) // 2, pl.ds(0, channels)]
            copies.append(
                pltpu.make_async_remote_copy(
                    src_ref=src, dst_ref=dst, send_sem=halo_send.at[n, i], recv_sem=halo_recv.at[n, i],
                    device_id=sides[i], device_id_type=MESH,
                )
            )
        return copies

    def send_all(g, first):
        src = row.at[g, pl.ds(0, 1)]
        for (a, b), peer in zip(PEERS, peers):
            if first:
                dst, done = grid.at[mx, pl.ds(my, 1)], all_recv.at[0]
            else:
                there = (-a % NGX, pl.ds(-b % NGY, 1))
                dst = (near if is_near(a, b) else far).at[(g, *there)]
                done = (all_recv if is_near(a, b) else far_recv).at[g]
            pltpu.make_async_remote_copy(
                src_ref=src, dst_ref=dst, send_sem=all_send.at[g], recv_sem=done,
                device_id=peer, device_id_type=MESH,
            ).start()
        mine = grid.at[mx, pl.ds(my, 1)] if first else near.at[g, 0, pl.ds(0, 1)]
        pltpu.make_async_copy(src, mine, all_recv.at[g]).start()
        pltpu.make_async_copy(src, junk.at[pl.ds(g, 1)], all_send.at[g]).start()

    def wait_rows(sem, count):
        part = junk.at[pl.ds(0, count)]
        pltpu.make_async_copy(part, part, sem).wait()

    def place(n, channel, target):
        for start, size, a in ((0, 12, 1), (12, 24, 0), (36, 12, -1)):
            low = arrive_y[n, SIDES.index((a, 1)), 0:size]
            high = arrive_y[n, SIDES.index((a, -1)), 0:size]
            low = pltpu.roll(low, TILE - 32 * channel, 1) if channel else low
            high = pltpu.roll(high, 96 - 32 * channel, 1) if channel < 3 else high
            middle = arrive_x[n, (a + 1) // 2, channel] if a else own[n, channel]
            lane = lax.broadcasted_iota(jnp.int32, (size, TILE), 1)
            target[PAD + start : PAD + start + size] = jnp.where(
                lane < 32, low, jnp.where(lane < 96, middle, high)
            )

    carry = {n: (hz < n if n > 0 else hz >= 8 + n) for n in (-3, -2, -1, 1, 2, 3)}

    def stage(total, k):
        wanted = combos(total)
        for block in range(ROWS // 8):
            r = PAD + 8 * block
            t = (rows8 + 8 * block) % 3
            middle = win[k, r : r + 8]
            up = jnp.where(t < 2, win[k, r + 1 : r + 9], win[k, r - 2 : r + 6])
            down = jnp.where(t > 0, win[k, r - 1 : r + 7], win[k, r + 2 : r + 10])
            for depth in sorted({nz for _, nz in wanted}):
                source = jnp.where(carry[depth], up if depth > 0 else down, middle) if depth else middle
                for ny, nz in wanted:
                    if nz == depth:
                        i = SLOT[ny, nz]
                        shifted[i, k, r : r + 8] = spread(source, lanes[SOURCE + i])

    def neighbour(o, k, r):
        nx, ny, nz = OFFSETS[o]
        i = SLOT[ny, nz]
        get = (lambda q: shifted[i, k, q : q + 8]) if (ny, nz) != (0, 0) else (lambda q: win[k, q : q + 8])
        if nx % 2 == 0:
            return get(r + 3 * (nx // 2))
        return jnp.where(odd, get(r + 3 * ((nx + 1) // 2)), get(r + 3 * ((nx - 1) // 2)))

    def pair(o, r, mine):
        delta = [
            (mine[k] - (0.5 * EDGE) * n) - neighbour(o, k, r) for k, n in enumerate(OFFSETS[o])
        ]
        square = delta[0] * delta[0] + delta[1] * delta[1] + delta[2] * delta[2]
        inverse = lax.rsqrt(square)
        return delta, square * inverse, inverse

    def masks(first, last):
        for block in range(BLOCKS):
            start = FIRST + 8 * block
            cell = (rows8 + start) // 3 % 4
            known = live_win[PAD + start : PAD + start + 8]
            over = {}
            for nx in range(-3, 4):
                dx = cell + (nx // 2 if nx % 2 == 0 else (nx - 1) // 2 + hz % 2)
                over[nx] = jnp.where(dx > 3, 9, jnp.where(dx < 0, -9, 0))
            for o in range(first, last):
                nx, ny, nz = OFFSETS[o]
                mask[o, 8 * block : 8 * block + 8] = spread(known, lanes[CODE + SLOT[ny, nz]] + over[nx])

    def step(n, total):
        for k in range(3):
            place(n, k, win.at[k])
        for k in range(3):
            stage(total, k)
        for block in range(BLOCKS):
            r = PAD + FIRST + 8 * block
            mine = [win[k, r : r + 8] for k in range(3)]
            density = zero8
            for o in range(total):
                delta, distance, inverse = pair(o, r, mine)
                gap = jnp.minimum(distance - RC, 0.0)
                live = mask[o, 8 * block : 8 * block + 8]
                held = live * gap
                density = density + held * gap
                if 0 < block < BLOCKS - 1:
                    close = jnp.minimum(distance - RP, 0.0)
                    quad = (2 * C0 - RP * C1) + distance * ((3 * C1 - 2 * RP * C2) + (4 * C2) * distance)
                    terms[o, block - 1, 0] = (close * quad) * (live * inverse)
                    terms[o, block - 1, 1] = held * inverse
                    for k in range(3):
                        terms[o, block - 1, 2 + k] = delta[k]
            win[3, r : r + 8] = -EMBED * lax.rsqrt(density)
        stage(total, 3)
        forces = []
        for block in range(OWN // 8):
            r = PAD + 12 + 8 * block
            slope = win[3, r : r + 8]
            total_force = [zero8] * 3
            for o in range(total):
                scalar = terms[o, block, 0] + (slope + neighbour(o, 3, r)) * terms[o, block, 1]
                total_force = [f - scalar * terms[o, block, 2 + k] for k, f in enumerate(total_force)]
            forces.append([jnp.where(inside, f, 0.0) for f in total_force])
        return forces

    def diffuse(t):
        for _ in range(SUB):
            beside = jnp.concatenate([t[1:], t[:1]], axis=0) + jnp.concatenate([t[-1:], t[:-1]], axis=0)
            beside = beside + pltpu.roll(t, 1, 1) + pltpu.roll(t, NGY - 1, 1)
            beside = beside + pltpu.roll(t, 1, 2) + pltpu.roll(t, TILE - 1, 2)
            t = t + RATE * (beside - 6.0 * t)
        return t

    def near_part(g, a, h, other):
        most = SUB - ring(a, NGX)
        within = rows8 <= most if h == 0 else rows8 >= 8 - most
        return jnp.where(within, near[g, a, 8 * h : 8 * h + 8], other)

    def weighed(get, marked):
        sums = [zero8] * (SUB + 1)
        for i, (c, a, h) in enumerate(TERMS):
            sums[c] = sums[c] + weigh[i] * get(a, h)
        if marked:
            sums = [jnp.where(lane8 == 1, 0.0, v) for v in sums]
        total = sums[0]
        for d in range(1, SUB + 1):
            total = total + (pltpu.roll(sums[d], d, 1) + pltpu.roll(sums[d], TILE - d, 1))
        return total

    def field_rows(a, h):
        return field[a, 8 * h : 8 * h + 8]

    def gathered_rows(g):
        return jnp.stack([
            jnp.concatenate([near_part(g, a, h, far[g, a, 8 * h : 8 * h + 8]) for h in range(2)], axis=0)
            for a in range(NGX)
        ])

    def deposit(g):
        lane3 = lax.broadcasted_iota(jnp.int32, (NGX, NGY, TILE), 2)
        added = jnp.where(lane3 == 1, 0.0, gathered_rows(g)) * (1.0 / HEAT)
        return diffuse(field[...] + added)

    def advance(n, forces):
        local = jnp.broadcast_to(jnp.sum(column[...], axis=0, keepdims=True), (8, TILE))
        power = []
        for block in range(OWN // 8):
            at = slice(8 * block, 8 * block + 8)
            push = jnp.sqrt((2.0 * MASS / DT) * spread(local, lanes[PLANE + block]))
            energy, places = zero8, []
            for k in range(3):
                speed = vel[k, at]
                speed = speed + (DT / MASS) * (forces[block][k] - MASS * speed + push * kick[n, k, at])
                vel[k, at] = speed
                moved = win[k, PAD + 12 + 8 * block : PAD + 20 + 8 * block] + DT * speed
                own[n + 1, k, at] = moved
                places.append(moved)
                energy = energy + speed * speed
            pack(n + 1, places, 8 * block, 8)
            power.append(energy)
        return power

    def energies(n, power):
        out = zero8
        index = [lanes[BACK] + (32 + 8 * i) for i in range(8)]
        for block in range(OWN // 8):
            parts = [spread(power[block], i) for i in index]
            while len(parts) > 1:
                parts = [a + b for a, b in zip(parts[::2], parts[1::2])]
            out = out + jnp.where(lanes[HELD + block] > 0, parts[0], 0.0)
        out = (MASS * DT) * jnp.sum(out, axis=0, keepdims=True)
        row[n + 1, 0:1] = jnp.where(lane8[0:1] == 1, top[0:1], out)

    def reach(n):
        most = zero8
        for block in range(OWN // 8):
            at = slice(8 * block, 8 * block + 8)
            square = sum(own[n + 1, k, at] * own[n + 1, k, at] for k in range(3))
            most = jnp.maximum(most, jnp.where(inside, square, 0.0))
        most = jnp.max(jnp.max(most, axis=1, keepdims=True), axis=0, keepdims=True)
        top[...] = jnp.broadcast_to(most, (8, TILE))

    def full_step(n, total):
        forces = step(n, total)

        @pl.when(n == 0)
        def _():
            wait_rows(all_recv.at[0], NGX * NGY)
            turn = jnp.transpose(grid[...].reshape(TILE, TILE)).reshape(NGX, NGY, TILE)
            grid_turned[...] = turn
            column[0:1] = grid_turned[mx, pl.ds(my, 1), :]
            column[1:8] = jnp.zeros((7, TILE), F32)

        @pl.when(n > 0)
        def _():
            wait_rows(all_recv.at[n], NEAR_ROWS)
            arrived = weighed(lambda a, h: near_part(n, a, h, 0.0), True)
            column[...] = column[...] + (1.0 / HEAT) * arrived

        power = advance(n, forces)

        @pl.when(n < STEPS - 1)
        def _():
            for c in halo_copies(n + 1, 3):
                c.start()

        energies(n, power)
        send_all(n + 1, False)

        reach(n)
        @pl.when(n == 0)
        def _():
            masks(NEAR, len(OFFSETS))
            for a in range(NGX):
                field[a] = pltpu.roll(grid_turned[gxs[a]], lax.rem(NGY - my, NGY), 0)

        @pl.when(n > 0)
        def _():
            wait_rows(far_recv.at[n], FAR_ROWS)
            field[...] = deposit(n)

        column[...] = weighed(field_rows, False)
        wait_rows(all_send.at[n], NGX * NGY)

        @pl.when(n < STEPS - 1)
        def _():
            waits = halo_copies(n + 1, 3)
            for c in waits:
                c.wait_recv()
            for c in waits:
                c.wait_send()

    first = halo_copies(0, 4)
    for c in first:
        c.start()
    send_all(0, True)
    for n in range(STEPS):
        for k in range(3):
            unpack(6 + 3 * n + k, kick.at[n, k])
    for c in first:
        c.wait_recv()
    for c in first:
        c.wait_send()

    place(0, 3, live_win)
    masks(0, NEAR)

    lax.fori_loop(0, 2, lambda n, c: (full_step(n, NEAR), c)[1], 0)
    lax.fori_loop(2, 4, lambda n, c: (full_step(n, len(OFFSETS)), c)[1], 0)

    for c in range(6):
        held = own.at[STEPS, c] if c < 3 else vel.at[c - 3]
        for cell in range(4):
            for ix in range(2):
                start = (4 * ix + cell) * 3
                raw[0, cell, 3 * ix : 3 * ix + 3] = held[start : start + 3]
        for iy in range(2):
            value = zero8
            for cell in range(4):
                part = raw[0, cell]
                part = part if cell == 1 + iy else pltpu.roll(part, (32 * (cell - 1 - iy)) % TILE, 1)
                value = jnp.where(lane8 // 32 == cell, part, value)
            back[iy, c] = value
    stores = [
        pltpu.make_async_copy(heat, heat_same, in_sem.at[1]),
        pltpu.make_async_copy(pairs, pairs_same, in_sem.at[0]),
        pltpu.make_async_copy(u_in, u_same, in_sem.at[15]),
        pltpu.make_async_copy(v_in, v_same, in_sem.at[16]),
    ]
    for ix in range(2):
        for iy in range(2):
            spot = pl.ds(3 * ix, 3)
            at = 3 + 3 * (2 * ix + iy)
            stores += [
                pltpu.make_async_copy(back.at[iy, pl.ds(0, 3), spot], u_out.at[:, ix, :, iy], in_sem.at[at]),
                pltpu.make_async_copy(back.at[iy, pl.ds(3, 3), spot], v_out.at[:, ix, :, iy], in_sem.at[at + 1]),
            ]
    for copy in stores:
        copy.start()
    lane1 = lane8[0:1] == 1
    wait_rows(all_recv.at[STEPS], NEAR_ROWS)
    wait_rows(far_recv.at[STEPS], FAR_ROWS)
    wait_rows(all_send.at[STEPS], NGX * NGY)
    most = [jnp.max(gathered_rows(g), axis=0) for g in range(2, STEPS + 1)]
    most = [jnp.max(v, axis=0, keepdims=True) for v in most]
    fine = (most[0] <= NEAR_LIMIT) & (jnp.maximum(most[1], most[2]) <= FAR_LIMIT)
    flag_out[0, 0] = jnp.sum(jnp.where(lane1 & fine, 1.0, 0.0))
    field[...] = deposit(STEPS)
    mine = lax.broadcasted_iota(jnp.int32, (NGY, TILE), 1) == mx * NGY + my
    planes = [jnp.where(mine, pltpu.roll(field[gxs_back[i]], my, 0), 0.0) for i in range(NGX)]
    heat_out[0] = jnp.sum(jnp.stack(planes), axis=2)
    for copy in stores:
        copy.wait()


def fast(displacement, velocity, noise, electron_temp, pair_list, pair_count):
    turn = lambda v: jnp.swapaxes(v, -3, -2)
    brick = (3, 2, TZ, 2, TILE)
    hbm = pl.BlockSpec(memory_space=pltpu.HBM)
    vmem = pl.BlockSpec(memory_space=pltpu.VMEM)
    total = len(OFFSETS)
    u, v, heat, flag, heat_same, pairs_same, u_same, v_same = pl.pallas_call(
        body,
        out_shape=(
            jax.ShapeDtypeStruct(brick, F32),
            jax.ShapeDtypeStruct(brick, F32),
            jax.ShapeDtypeStruct((1, NGX, NGY), F32),
            jax.ShapeDtypeStruct((1, 1), F32),
            jax.ShapeDtypeStruct((NGX, NGY), F32),
            jax.ShapeDtypeStruct((2, PAIRS), jnp.int32),
            jax.ShapeDtypeStruct(brick, F32),
            jax.ShapeDtypeStruct(brick, F32),
        ),
        in_specs=[hbm] * 6,
        out_specs=(hbm, hbm, vmem, pl.BlockSpec(memory_space=pltpu.SMEM), hbm, hbm, hbm, hbm),
        scratch_shapes=[
            pltpu.VMEM((STEPS + 1, 4, OWN, TILE), F32),
            pltpu.VMEM((STEPS + 1, 2, OWN, TILE), F32),
            pltpu.VMEM((STEPS, 2, 4, 12, TILE), F32),
            pltpu.VMEM((STEPS, 8, OWN, TILE), F32),
            pltpu.VMEM((8, TILE), F32),
            pltpu.VMEM((NGX, NGY, TILE), F32),
            pltpu.VMEM((NGX, NGY, TILE), F32),
            pltpu.VMEM((STEPS + 1, NGX, NGY, TILE), F32),
            pltpu.VMEM((STEPS + 1, NGX, NGY, TILE), F32),
            pltpu.VMEM((len(TERMS), 8, TILE), F32),
            pltpu.VMEM((8, TILE), F32),
            pltpu.VMEM((STEPS + 1, 8, TILE), F32),
            pltpu.VMEM((4, FLAT, TILE), F32),
            pltpu.VMEM((len(SHIFTS), 4, FLAT, TILE), F32),
            pltpu.VMEM((total, 8 * BLOCKS, TILE), F32),
            pltpu.VMEM((total, OWN // 8, 5, 8, TILE), F32),
            pltpu.VMEM((FLAT, TILE), F32),
            pltpu.VMEM((3, OWN, TILE), F32),
            pltpu.VMEM((STEPS, 3, OWN, TILE), F32),
            pltpu.VMEM((NGX, NGY, TILE), F32),
            pltpu.VMEM((2, 18, 8, TILE), F32),
            pltpu.VMEM((2, 6, 8, TILE), F32),
            pltpu.VMEM((NGX, NGY), F32),
            pltpu.VMEM((2, PAIRS), jnp.int32),
            pltpu.SMEM((1, 1), jnp.int32),
            pltpu.VMEM((TABLES, 8, TILE), jnp.int32),
            pltpu.SemaphoreType.DMA((15 + 4 * STEPS,)),
            pltpu.SemaphoreType.DMA((STEPS, 8)),
            pltpu.SemaphoreType.DMA((STEPS, 8)),
            pltpu.SemaphoreType.DMA((STEPS + 1,)),
            pltpu.SemaphoreType.DMA((STEPS + 1,)),
            pltpu.SemaphoreType.DMA((STEPS + 1,)),
            pltpu.VMEM((NGX * NGY, TILE), F32),
        ],
        compiler_params=pltpu.CompilerParams(
            collective_id=0, has_side_effects=True, vmem_limit_bytes=60 << 20
        ),
    )(turn(displacement), turn(velocity), turn(noise), electron_temp[0], pair_list[0, 0], pair_count)
    return (turn(u), turn(v), heat), flag, (turn(u_same), turn(v_same), heat_same[None], pairs_same[None, None])


def padded_2(values, sides, width):
    for axis, dim in sides:
        count = lax.axis_size(axis)
        forward = [(i, (i + 1) % count) for i in range(count)]
        backward = [(target, source) for source, target in forward]
        low = lax.ppermute(lax.slice_in_dim(values, values.shape[dim] - width, None, axis=dim), axis, forward)
        high = lax.ppermute(lax.slice_in_dim(values, 0, width, axis=dim), axis, backward)
        values = jnp.concatenate([low, values, high], axis=dim)
    return values


def lattice_sites():
    serial = jnp.arange(TILE, dtype=jnp.int32)
    cell = serial // 2
    corners = jnp.stack([cell // 16, cell // 4 % 4, cell % 4])
    return EDGE * (corners.astype(F32) + ((serial % 2).astype(F32) * 0.5)[None, :])


def pair_geometry(flat, tile_index, code, lattice):
    t, iy, ix = tile_index % TZ, tile_index // TZ % 2, tile_index // (TZ * 2)
    ex, ey, ez = code // 9, code // 3 % 3, code % 3
    own_index = ((ix + 1) * 4 + iy + 1) * TZ + t
    other_index = ((ix + ex) * 4 + iy + ey) * TZ + (t + ez - 1 + TZ) % TZ
    own_tile = lax.dynamic_index_in_dim(flat, own_index, 1, keepdims=False)
    other_tile = lax.dynamic_index_in_dim(flat, other_index, 1, keepdims=False)
    offset = jnp.stack([ex - 1, ey - 1, ez - 1]).astype(F32) * (4 * EDGE)
    delta = (lattice + own_tile)[:, :, None] - (lattice + other_tile + offset[:, None])[:, None, :]
    square = jnp.sum(delta * delta, axis=0)
    serial = jnp.arange(TILE, dtype=jnp.int32)
    same = (code == 13) & (serial[:, None] == serial[None, :])
    return delta, jnp.sqrt(jnp.where(same, 100.0, square)), own_index, other_index


def density_term(flat, lattice, tile_index, code):
    _, distance, _, _ = pair_geometry(flat, tile_index, code, lattice)
    gap = distance - RC
    return jnp.sum(jnp.where(distance < RC, gap * gap, 0.0), axis=1)[None]


def force_term(flat, embed, lattice, tile_index, code):
    delta, distance, own_index, other_index = pair_geometry(flat, tile_index, code, lattice)
    own_embed = lax.dynamic_index_in_dim(embed, own_index, 0, keepdims=False)
    other_embed = lax.dynamic_index_in_dim(embed, other_index, 0, keepdims=False)
    gap = distance - RP
    poly = C0 + C1 * distance + C2 * distance * distance
    slope = jnp.where(distance < RP, 2.0 * gap * poly + gap * gap * (C1 + 2.0 * C2 * distance), 0.0)
    dens = jnp.where(distance < RC, 2.0 * (distance - RC), 0.0)
    scalar = (slope + (own_embed[:, None] + other_embed[None, :]) * dens) / distance
    return -jnp.sum(scalar[None] * delta, axis=2)


def sweep(term, channels, table, total):
    def visit(i, running):
        entry = lax.dynamic_slice_in_dim(table, i, 1, 1)
        u = entry[0, 0]
        value = jnp.where(i < total, term(u, entry[1, 0]), 0.0)
        old = lax.dynamic_slice_in_dim(running, u, 1, 1)
        return lax.dynamic_update_slice_in_dim(running, old + value[:, None], u, 1)

    running = lax.fori_loop(0, PAIRS, visit, jnp.zeros((channels, TILES, TILE), F32))
    return running.reshape(channels, 2, 2, TZ, TILE)


def slow(displacement, velocity, noise, electron_temp, pair_list, pair_count):
    lattice = lattice_sites()
    table, total = pair_list[0, 0], pair_count[0, 0]
    owners = NGX * NGY
    serial = np.arange(TZ * TILE)
    layer = serial // TILE * 8 + serial % 8
    onehot = jnp.asarray((layer * owners // 24)[:, None] == np.arange(owners)[None, :])
    axes = (("gx", 1), ("gy", 2))

    def one(n, carry):
        positions, speeds, heat = carry
        arrived = lax.all_to_all(heat.reshape(1, owners), ("gx", "gy"), split_axis=1, concat_axis=0, tiled=True)
        local = jnp.sum(jnp.where(onehot, arrived.reshape(1, owners), 0.0), axis=1).reshape(1, 1, 1, TZ, TILE)
        flat = padded_2(positions, axes, 1).reshape(3, 16 * TZ, TILE)
        density = sweep(partial(density_term, flat, lattice), 1, table, total)
        embed = padded_2(-EMBED / (2.0 * jnp.sqrt(density)), axes, 1).reshape(16 * TZ, TILE)
        force = sweep(partial(force_term, flat, embed, lattice), 3, table, total)
        kicker = jnp.sqrt(2.0 * MASS * local / DT) * lax.dynamic_index_in_dim(noise, n, 0, keepdims=False)
        speeds = speeds + DT / MASS * (force - MASS * speeds + kicker)
        positions = positions + DT * speeds
        power = MASS * DT * jnp.sum(speeds * speeds, axis=0)
        power = jnp.sum(power, axis=(0, 1)).reshape(-1, 1)
        energy = jnp.sum(jnp.where(onehot, power, 0.0), axis=0)
        arrived = lax.all_to_all(energy.reshape(owners, 1), ("gx", "gy"), split_axis=0, concat_axis=1, tiled=True)
        heat = heat + arrived.reshape(1, NGX, NGY) / HEAT

        def relax(_, heat):
            padded = padded_2(heat, ((("gx", "gy"), 0),), 1)
            beside = padded[2:] + padded[:-2] + jnp.roll(heat, 1, 1) + jnp.roll(heat, -1, 1)
            beside = beside + jnp.roll(heat, 1, 2) + jnp.roll(heat, -1, 2)
            return heat + RATE * (beside - 6.0 * heat)

        return positions, speeds, lax.fori_loop(0, SUB, relax, heat)

    return lax.fori_loop(0, STEPS, one, (displacement, velocity, electron_temp))


def per_device(*arguments):
    results, flag, (displacement, velocity, heat, pairs) = fast(*arguments)
    noise, count = arguments[2], arguments[5]
    return lax.cond(
        flag[0, 0] > 0.5, lambda: results, lambda: slow(displacement, velocity, noise, heat, pairs, count)
    )


def solution(mesh):
    brick = P(None, "gx", "gy", None, None)
    placed = (
        brick,
        brick,
        P(None, None, "gx", "gy", None, None),
        P(("gx", "gy"), None, None),
        P("gx", "gy", None, None),
        P("gx", "gy"),
    )
    return jax.shard_map(
        per_device, mesh=mesh, in_specs=placed, out_specs=(brick, brick, P(("gx", "gy"), None, None)), check_vma=False
    )
```
